32 devices in a mesh: dp: 8 (over z, y), group: 4 (over x, core).
Axes of the slice: x: 2, y: 2, z: 4, core: 2. Of those that a mesh axis runs over, the one named last changes fastest.
Arguments:
- waveform: bfloat16 [128, 2560], P(('dp', 'group')), may hold values from -6 to 6
- lengths: int32 [128], P(('dp', 'group')), may hold values from 1280 to 2560
- packing: int32 [128], P(('dp', 'group')), may hold values from 0 to 15, as said below
- first_weight: bfloat16 [512, 10], P('dp'), may hold values from -2 to 2
- norm_gain: float32 [512], replicated, may hold values from 0.25 to 1.75
- norm_bias: float32 [512], replicated, may hold values from -3 to 3
- conv_weight: bfloat16 [512, 1536], P('dp'), may hold values from -0.15625 to 0.15625
- grad_features: bfloat16 [128, 255, 512], P(('dp', 'group')), may hold values from -0.25 to 0.25
Outputs:
- features: bfloat16 [128, 255, 512], P(('dp', 'group'))
- grad_conv: float32 [512, 1536], P('dp')
- grad_first: float32 [512, 10], P('dp')
- grad_gain: float32 [512], replicated
- grad_bias: float32 [512], replicated
The draws below stay inside these ranges and needn't reach their ends.
Inputs may be any that keep to these rules, and one draw needn't show every extreme that they name: `packing`: within each index of dp the 16 rows form a permutation of the positions of that index's block; position p lies on the device of group index p // 4 of the same dp index. Each device sends an even number of its rows to each device of its group, at most 2 to one device, and exactly 2 to some.
All inputs are finite; a program needn't handle non-finite values.
Results may differ from the reference program's by a relative error of at most 0.0057.
Values may be sent and summed in bfloat16 or wider, within the bound.
A program may use at most 64 MiB of HBM per device.

```python
import jax
import jax.numpy as jnp
from jax import lax

C = 512
CAP = 2560
ROWS_DEV = 4
F1 = 255
UTTS = 128
N_DP = 8
N_GROUP = 4


def draw_packing(key, part):
    block_rows = N_GROUP * ROWS_DEV
    key_rows, key_offset, key_label, key_slot = jax.random.split(key, 4)
    row_order = jax.vmap(lambda sub: jax.random.permutation(sub, ROWS_DEV))(jax.random.split(key_rows, N_DP * N_GROUP))
    row_order = row_order.reshape(N_DP, N_GROUP, ROWS_DEV)
    shift_amount = row_order // 2 % N_GROUP
    offset = jax.random.randint(key_offset, (N_DP, 1, 1), 0, N_GROUP)
    relabel = jax.vmap(lambda sub: jax.random.permutation(sub, N_GROUP))(jax.random.split(key_label, N_DP))
    source = jnp.arange(N_GROUP)[None, :, None]
    cycled = (source + shift_amount + offset) % N_GROUP
    target = jnp.take_along_axis(relabel, cycled.reshape(N_DP, block_rows), axis=1)
    positions = jnp.arange(block_rows)
    same_target = target[:, :, None] == target[:, None, :]
    earlier = positions[:, None] > positions[None, :]
    rank_among = jnp.sum((same_target & earlier[None]).astype(jnp.int32), axis=2)
    slot_perm = jax.vmap(lambda sub: jax.random.permutation(sub, ROWS_DEV))(jax.random.split(key_slot, N_DP * N_GROUP))
    slot_perm = slot_perm.reshape(N_DP, block_rows)
    slot_value = jnp.take_along_axis(slot_perm, target * ROWS_DEV + rank_among, axis=1)
    return (target * ROWS_DEV + slot_value).reshape(N_DP * block_rows).astype(jnp.int32)


def touch_ends(entries, own_key, low, largest):
    spot = [jax.random.randint(jax.random.fold_in(own_key, axis), (), 0, length) for axis, length in enumerate(entries.shape)]
    main_axis = entries.shape.index(max(entries.shape))
    neighbour = spot[:main_axis] + [(spot[main_axis] + 1) % entries.shape[main_axis]] + spot[main_axis + 1:]
    return entries.at[tuple(spot)].set(low).at[tuple(neighbour)].set(largest)


def strengthened(drawn, rng, source, target, parts, factor):
    def block_of(dim):
        return (jnp.arange(drawn.shape[dim]) // (drawn.shape[dim] // parts)).reshape((-1,) + (1,) * (drawn.ndim - 1 - dim))

    first = jax.random.permutation(rng, parts)[block_of(target)]
    other_side = (block_of(target) + parts // 2) % parts
    return jnp.where((block_of(source) == first) | (block_of(source) == other_side), factor * drawn, drawn)


def levels(own_key, shape, cuts, smallest, largest):
    gain, own = 1.0, jax.random.fold_in(own_key, 6)
    for axis_at, parts in cuts:
        draws = jnp.exp(jax.random.uniform(jax.random.fold_in(own, axis_at), (parts,), jnp.float32, smallest / len(cuts), largest / len(cuts)))
        gain = gain * jnp.repeat(draws, shape[axis_at] // parts).reshape([-1 if axis == axis_at else 1 for axis in range(len(shape))])
    return gain


def gaussian(own_key, extent, width, bound, shards=(), kind=jnp.bfloat16):
    entries = jax.random.normal(own_key, extent, jnp.float32) * width
    if len(shards) > 0:
        entries = levels(own_key, extent, shards, -0.22, 0.18) * entries
    return jnp.clip(entries, min=-bound, max=bound).astype(kind)


def gaussian_with(stream_key, shape, spread, bound, pieces, heavy, held_as=jnp.bfloat16):
    values = spread * jax.random.normal(stream_key, shape, jnp.float32)
    if pieces:
        values = values * levels(stream_key, shape, pieces, -0.22, 0.18)
    return jnp.clip(strengthened(values, jax.random.fold_in(stream_key, 3), *heavy), -bound, bound).astype(held_as)


def setup_inputs(seed: int = 0) -> dict:
    streams_of = jax.random.split(jax.random.key(seed), 9)
    waveform = gaussian(streams_of[0], (UTTS, CAP), 1.0, 6.0, ((0, 32),))
    lengths = touch_ends(jax.random.randint(streams_of[1], (UTTS,), CAP // 2, CAP + 1), jax.random.fold_in(streams_of[1], 1), CAP // 2, CAP).astype(jnp.int32)
    packing = draw_packing(jax.random.fold_in(streams_of[8], 71), 0)
    first_weight = gaussian(streams_of[3], (C, 10), 10 ** -0.5, 2.0, ((0, 8),))
    norm_gain = jnp.clip(1.0 + 0.15 * jax.random.normal(streams_of[4], (C,), jnp.float32), 0.25, 1.75)
    norm_bias = gaussian(streams_of[5], (C,), 0.5, 3.0, (), jnp.float32)
    conv_weight = gaussian(streams_of[6], (C, 3 * C), (3 * C) ** -0.5, 0.15625, ((0, 8),))
    grad_features = gaussian_with(streams_of[7], (UTTS, F1, C), (4.0 * (UTTS * F1) ** -0.5), 0.25, ((0, 32),), (0, 2, 32, 2.75))
    return {"waveform": waveform, "lengths": lengths, "packing": packing, "first_weight": first_weight, "norm_gain": norm_gain, "norm_bias": norm_bias, "conv_weight": conv_weight, "grad_features": grad_features}


def gelu_slope(values):
    return 0.5 * (1.0 + lax.erf(values * 0.7071067811865476)) + values * jnp.exp(-0.5 * values * values) * 0.3989422804014327

def tap_matrix(hidden, frames_second):
    row_count, frames_first, channels = hidden.shape
    zero_frame = jnp.zeros((row_count, 1, channels), hidden.dtype)
    paired = jnp.concatenate([hidden, zero_frame], axis=1).reshape(row_count, frames_second + 1, 2, channels)
    even_half = paired[:, :, 0]
    odd_half = paired[:, :, 1]
    stacked = jnp.concatenate([even_half[:, :frames_second], odd_half[:, :frames_second], even_half[:, 1:]], axis=2)
    return stacked.reshape(row_count * frames_second, 3 * channels)

def spread_back(back_taps, row_count, frames_second, frames_first):
    first_tap = back_taps[0].reshape(row_count, frames_second, -1)
    middle_tap = back_taps[1].reshape(row_count, frames_second, -1)
    last_tap = back_taps[2].reshape(row_count, frames_second, -1)
    channels = first_tap.shape[2]
    zero_frame = jnp.zeros((row_count, 1, channels), jnp.float32)
    even_half = jnp.concatenate([first_tap, zero_frame], axis=1) + jnp.concatenate([zero_frame, last_tap], axis=1)
    odd_half = jnp.concatenate([middle_tap, zero_frame], axis=1)
    joined = jnp.stack([even_half, odd_half], axis=2).reshape(row_count, 2 * frames_second + 2, channels)
    return joined[:, :frames_first]

def encode_block(wave_rows, row_lengths, first_weight, norm_gain, norm_bias, conv_weight, cotangent):
    row_count, capacity = wave_rows.shape
    channels = norm_gain.shape[0]
    frames_first = capacity // 5 - 1
    frames_second = (capacity // 5 - 2) // 2
    in_length = jnp.arange(capacity)[None, :] < row_lengths[:, None]
    masked = jnp.where(in_length, wave_rows, jnp.zeros_like(wave_rows))
    blocks = masked.reshape(row_count, capacity // 5, 5)
    taps_first = jnp.concatenate([blocks[:, :-1], blocks[:, 1:]], axis=2).reshape(row_count * frames_first, 10)
    conv_first = lax.dot_general(taps_first, first_weight, (((1,), (1,)), ((), ())), preferred_element_type=jnp.float32)
    conv_first = conv_first.reshape(row_count, frames_first, channels)
    count_first = (row_lengths - 10) // 5 + 1
    count_second = (count_first - 3) // 2 + 1
    valid_first = (jnp.arange(frames_first)[None, :] < count_first[:, None]).astype(jnp.float32)[:, :, None]
    valid_second = (jnp.arange(frames_second)[None, :] < count_second[:, None]).astype(jnp.float32)[:, :, None]
    count_float = count_first.astype(jnp.float32)[:, None, None]
    row_mean = lax.optimization_barrier(jnp.sum(conv_first * valid_first, axis=1, keepdims=True)) / count_float
    centred = (conv_first - row_mean) * valid_first
    row_var = lax.optimization_barrier(jnp.sum(centred * centred, axis=1, keepdims=True)) / count_float
    inv_scale = lax.rsqrt(row_var + 1e-05)
    normed = (conv_first - row_mean) * inv_scale
    shifted = normed * norm_gain + norm_bias
    hidden = (jax.nn.gelu(shifted, approximate=False) * valid_first).astype(jnp.bfloat16)
    taps_second = tap_matrix(hidden, frames_second)
    conv_second = lax.dot_general(taps_second, conv_weight, (((1,), (1,)), ((), ())), preferred_element_type=jnp.float32)
    conv_second = conv_second.reshape(row_count, frames_second, channels)
    features = (jax.nn.gelu(conv_second, approximate=False) * valid_second).astype(jnp.bfloat16)
    delta_second = (cotangent.astype(jnp.float32) * valid_second * gelu_slope(conv_second)).astype(jnp.bfloat16)
    delta_flat = delta_second.reshape(row_count * frames_second, channels)
    grad_conv = lax.dot_general(delta_flat, taps_second, (((0,), (0,)), ((), ())), preferred_element_type=jnp.float32)
    back_taps = tuple((jnp.dot(delta_flat, conv_weight[:, tap_index * channels:(tap_index + 1) * channels], preferred_element_type=jnp.float32) for tap_index in range(3)))
    delta_hidden = spread_back(back_taps, row_count, frames_second, frames_first)
    delta_norm = delta_hidden * valid_first * gelu_slope(shifted)
    grad_gain = lax.optimization_barrier(jnp.sum(delta_norm * normed, axis=(0, 1)))
    grad_bias = lax.optimization_barrier(jnp.sum(delta_norm, axis=(0, 1)))
    scaled = delta_norm * norm_gain
    mean_grad = lax.optimization_barrier(jnp.sum(scaled, axis=1, keepdims=True)) / count_float
    mean_cross = lax.optimization_barrier(jnp.sum(scaled * normed, axis=1, keepdims=True)) / count_float
    delta_first = ((scaled - mean_grad - normed * mean_cross) * inv_scale * valid_first).astype(jnp.bfloat16)
    grad_first = lax.dot_general(delta_first.reshape(row_count * frames_first, channels), taps_first, (((0,), (0,)), ((), ())), preferred_element_type=jnp.float32)
    return (features, grad_conv, grad_first, grad_gain, grad_bias)

def reference(waveform, lengths, packing, first_weight, norm_gain, norm_bias, conv_weight, grad_features):
    block_rows = N_GROUP * ROWS_DEV
    wave_blocks = waveform.reshape(N_DP, block_rows, CAP)
    length_blocks = lengths.reshape(N_DP, block_rows)
    pack_blocks = packing.reshape(N_DP, block_rows)
    cot_blocks = grad_features.reshape(N_DP, block_rows, F1, C)

    def block_step(carry, inputs):
        wave_rows, row_lengths, pack_rows, cotangent = inputs
        packed_wave = jnp.zeros_like(wave_rows).at[pack_rows].set(wave_rows)
        packed_lengths = jnp.zeros_like(row_lengths).at[pack_rows].set(row_lengths)
        features, grad_conv, grad_first, grad_gain, grad_bias = encode_block(packed_wave, packed_lengths, first_weight, norm_gain, norm_bias, conv_weight, cotangent)
        return ((carry[0] + grad_conv, carry[1] + grad_first, carry[2] + grad_gain, carry[3] + grad_bias), features)
    start = (jnp.zeros((C, 3 * C), jnp.float32), jnp.zeros((C, 10), jnp.float32), jnp.zeros((C,), jnp.float32), jnp.zeros((C,), jnp.float32))
    totals, features = lax.scan(block_step, start, (wave_blocks, length_blocks, pack_blocks, cot_blocks))
    return (features.reshape(UTTS, F1, C), totals[0], totals[1], totals[2], totals[3])
```

```python
import functools

import jax
import jax.numpy as jnp
from jax import lax
from jax.experimental import pallas as pl
from jax.experimental.pallas import tpu as pltpu
from jax.sharding import PartitionSpec as P

MESH = pl.DeviceIdType.MESH
F32, BF16 = jnp.float32, jnp.bfloat16
CHUNK = 32


def gelu_slope(values):
    return (
        0.5 * (1.0 + lax.erf(values * 0.7071067811865476))
        + values * jnp.exp(-0.5 * values * values) * 0.3989422804014327
    )


def tap_matrix(hidden, frames_second):
    row_count, frames_first, channels = hidden.shape
    zero_frame = jnp.zeros((row_count, 1, channels), hidden.dtype)
    paired = jnp.concatenate([hidden, zero_frame], axis=1).reshape(
        row_count, frames_second + 1, 2, channels
    )
    even_half = paired[:, :, 0]
    odd_half = paired[:, :, 1]
    stacked = jnp.concatenate(
        [even_half[:, :frames_second], odd_half[:, :frames_second], even_half[:, 1:]], axis=2
    )
    return stacked.reshape(row_count * frames_second, 3 * channels)


def spread_back(back_taps, row_count, frames_second, frames_first):
    first_tap = back_taps[0].reshape(row_count, frames_second, -1)
    middle_tap = back_taps[1].reshape(row_count, frames_second, -1)
    last_tap = back_taps[2].reshape(row_count, frames_second, -1)
    channels = first_tap.shape[2]
    zero_frame = jnp.zeros((row_count, 1, channels), jnp.float32)
    even_half = jnp.concatenate([first_tap, zero_frame], axis=1) + jnp.concatenate(
        [zero_frame, last_tap], axis=1
    )
    odd_half = jnp.concatenate([middle_tap, zero_frame], axis=1)
    joined = jnp.stack([even_half, odd_half], axis=2).reshape(
        row_count, 2 * frames_second + 2, channels
    )
    return joined[:, :frames_first]


def local(
    waveform, lengths, packing, first_weight, norm_gain, norm_bias, conv_weight, grad_features
):
    row_count, capacity = waveform.shape
    channels = norm_gain.shape[0]
    frames_first = capacity // 5 - 1
    frames_second = (capacity // 5 - 2) // 2
    groups = lax.axis_size("group")
    own_group = lax.axis_index("group")
    group_rows = groups * row_count
    all_pack, all_lengths = (
        lax.all_gather(packing, "group", axis=0, tiled=True),
        lax.all_gather(lengths, "group", axis=0, tiled=True),
    )
    target = all_pack // row_count
    slot_index = all_pack % row_count
    positions = jnp.arange(group_rows)
    source = positions // row_count
    same_source = source[:, None] == source[None, :]
    same_target = target[:, None] == target[None, :]
    before = positions[:, None] > positions[None, :]
    rank_among = jnp.sum((same_source & same_target & before).astype(jnp.int32), axis=1)
    arriving = target == own_group
    slot_ids = jnp.arange(row_count)
    choose_slot = (slot_index[None, :] == slot_ids[:, None]) & arriving[None, :]
    local_lengths = jnp.sum(jnp.where(choose_slot, all_lengths[None, :], 0), axis=1)
    per_peer = 2 * ((row_count + 2 * groups - 1) // (2 * groups))
    lane_ids = jnp.arange(per_peer)
    own_target = lax.dynamic_slice_in_dim(target, own_group * row_count, row_count)
    own_rank = lax.dynamic_slice_in_dim(rank_among, own_group * row_count, row_count)
    outgoing = (
        (own_target[None, None, :] == jnp.arange(groups)[:, None, None])
        & (own_rank[None, None, :] == lane_ids[None, :, None])
    ).astype(jnp.bfloat16)
    send_rows = jnp.einsum(
        "gkr,rs->gks", outgoing, waveform, preferred_element_type=jnp.float32
    ).astype(jnp.bfloat16)
    received = lax.all_to_all(send_rows, "group", split_axis=0, concat_axis=0, tiled=True)
    pick_slots = (
        choose_slot[:, :, None] & (rank_among[None, :, None] == lane_ids[None, None, :])
    ).astype(jnp.float32)
    pick_slots = jnp.sum(pick_slots.reshape(row_count, groups, row_count, per_peer), axis=2).astype(
        jnp.bfloat16
    )
    wave_rows = jnp.einsum(
        "lsk,skn->ln", pick_slots, received, preferred_element_type=jnp.float32
    ).astype(jnp.bfloat16)
    first_whole = lax.all_gather(first_weight, "dp", axis=0, tiled=True)
    in_length = jnp.arange(capacity)[None, :] < local_lengths[:, None]
    masked = jnp.where(in_length, wave_rows, jnp.zeros_like(wave_rows))
    blocks = masked.reshape(row_count, capacity // 5, 5)
    taps_first = jnp.concatenate([blocks[:, :-1], blocks[:, 1:]], axis=2).reshape(
        row_count * frames_first, 10
    )
    conv_first = lax.dot_general(
        taps_first, first_whole, (((1,), (1,)), ((), ())), preferred_element_type=jnp.float32
    )
    conv_first = conv_first.reshape(row_count, frames_first, channels)
    count_first = (local_lengths - 10) // 5 + 1
    count_second = (count_first - 3) // 2 + 1
    valid_first = (jnp.arange(frames_first)[None, :] < count_first[:, None]).astype(jnp.float32)[
        :, :, None
    ]
    valid_second = (jnp.arange(frames_second)[None, :] < count_second[:, None]).astype(jnp.float32)[
        :, :, None
    ]
    count_float = count_first.astype(jnp.float32)[:, None, None]
    row_mean = jnp.sum(conv_first * valid_first, axis=1, keepdims=True) / count_float
    centred = (conv_first - row_mean) * valid_first
    row_var = jnp.sum(centred * centred, axis=1, keepdims=True) / count_float
    inv_scale = lax.rsqrt(row_var + 1e-05)
    normed = (conv_first - row_mean) * inv_scale
    shifted = normed * norm_gain + norm_bias
    hidden = (jax.nn.gelu(shifted, approximate=False) * valid_first).astype(jnp.bfloat16)
    taps_second = tap_matrix(hidden, frames_second)
    conv_whole = lax.all_gather(conv_weight, "dp", axis=0, tiled=True)
    conv_second = lax.dot_general(
        taps_second, conv_whole, (((1,), (1,)), ((), ())), preferred_element_type=jnp.float32
    )
    conv_second = conv_second.reshape(row_count, frames_second, channels)
    features = (jax.nn.gelu(conv_second, approximate=False) * valid_second).astype(jnp.bfloat16)
    delta_second = (
        grad_features.astype(jnp.float32) * valid_second * gelu_slope(conv_second)
    ).astype(jnp.bfloat16)
    delta_flat = delta_second.reshape(row_count * frames_second, channels)
    back_taps = tuple(
        (
            jnp.dot(
                delta_flat,
                conv_whole[:, tap_index * channels : (tap_index + 1) * channels],
                preferred_element_type=jnp.float32,
            )
            for tap_index in range(3)
        )
    )
    share = lax.psum_scatter(
        lax.dot_general(
            delta_flat, taps_second, (((0,), (0,)), ((), ())), preferred_element_type=jnp.float32
        ),
        "dp",
        scatter_dimension=0,
        tiled=True,
    )
    grad_conv = lax.psum(share, "group")
    delta_hidden = spread_back(back_taps, row_count, frames_second, frames_first)
    delta_norm = delta_hidden * valid_first * gelu_slope(shifted)
    gain_term = jnp.sum(delta_norm * normed, axis=(0, 1))
    bias_term = jnp.sum(delta_norm, axis=(0, 1))
    scaled = delta_norm * norm_gain
    mean_grad = jnp.sum(scaled, axis=1, keepdims=True) / count_float
    mean_cross = jnp.sum(scaled * normed, axis=1, keepdims=True) / count_float
    delta_first = ((scaled - mean_grad - normed * mean_cross) * inv_scale * valid_first).astype(
        jnp.bfloat16
    )
    first_term = lax.dot_general(
        delta_first.reshape(row_count * frames_first, channels),
        taps_first,
        (((0,), (0,)), ((), ())),
        preferred_element_type=jnp.float32,
    )
    stacked = jnp.concatenate([first_term, gain_term[:, None], bias_term[:, None]], axis=1)
    summed = lax.psum(stacked, ("dp", "group"))
    shard_rows = channels // lax.axis_size("dp")
    grad_first = lax.dynamic_slice_in_dim(
        summed[:, :10], lax.axis_index("dp") * shard_rows, shard_rows, 0
    )
    return (features, grad_conv, grad_first, summed[:, 10], summed[:, 11])


BLOCKS = ((0, 512), (512, 512), (1024, 512))


def phi_and_slope(values):
    phi = 0.5 + 0.5 * lax.erf(values * 0.7071067811865476)
    return phi, phi + (values * 0.3989422804014327) * jnp.exp2(values * values * -0.7213475204444817)


def fold_rows(block):
    return jnp.sum(block.reshape(block.shape[0] // 8, 8, block.shape[1]), axis=0)


def three_parts(values, out):
    high = values.astype(BF16)
    rest = values - high.astype(F32)
    middle = rest.astype(BF16)
    out[0:16] = high
    out[16:32] = middle
    out[32:48] = (rest - middle.astype(F32)).astype(BF16)


def fused_kernel(
    wave_ref, first_ref, conv_ref, gain_ref, bias_ref, cot_ref,
    feat_ref, gconv_ref, gfirst_ref, ggain_ref, gbias_ref,
    rows_all, first_all, first16, conv_all, turned, slope, taps, even_rows, delta, before, delta_turned,
    cot_wide, cot_rows, feat_wide, feat_rows, lhs_even, lhs_odd, rhs, counts, means, inv_all, gram, cross, acc,
    gc_full, gc_send, gc_r1, gc_k2, gc_s2, gc_r2, gc_k3, gc_s3, gc_r3, gc_out,
    sm_half, sm_core, sm_xy, sm_z, sm_out,
    row_ss, row_rs, first_ss, first_rs, own_ss, yfw_ss, xfw_ss, cfw_ss, conv_rs, own_sem, cot_sem, feat_sem,
    s1_ss, s1_rs, s2_ss, s2_rs, s3_ss, s3_rs, s4_ss, s4_rs,
    sc_ss, sc_rs, sxy_ss, sxy_rs, sz_ss, sz_rs, so_ss, so_rs,
):
    dp, grp = lax.axis_index("dp"), lax.axis_index("group")
    core, xpos = grp % 2, grp // 2
    ypos, zpos = dp % 2, dp // 2
    partner = (dp, xpos * 2 + (1 - core))
    xpeer = (dp, (1 - xpos) * 2 + core)
    ypeer = (zpos * 2 + (1 - ypos), grp)
    corner = (zpos * 2 + (1 - ypos), (1 - xpos) * 2 + core)
    plane = (None, xpeer, ypeer, corner)

    def zpeer(j):
        return ((zpos + j) % 4) * 2 + ypos

    def remote(src, dst, ss, rs, dev):
        return pltpu.make_async_remote_copy(
            src_ref=src, dst_ref=dst, send_sem=ss, recv_sem=rs, device_id=dev, device_id_type=MESH
        )

    sends = []

    def send(src, dst, ss, rs, dev):
        c = remote(src, dst, ss, rs, dev)
        c.start()
        sends.append(c)

    def arrived(ref, ss, rs, dev):
        remote(ref, ref, ss, rs, dev).wait_recv()

    cot_in = pltpu.make_async_copy(cot_ref, cot_wide.at[0:255], cot_sem)
    barrier = pltpu.get_barrier_semaphore()
    for j in range(1, 4):
        pl.semaphore_signal(barrier, inc=1, device_id=(dp, (grp + j) % 4), device_id_type=MESH)
    for j in range(1, 8):
        pl.semaphore_signal(barrier, inc=1, device_id=((dp + j) % 8, grp), device_id_type=MESH)
    pl.semaphore_signal(barrier, inc=1, device_id=corner, device_id_type=MESH)
    own = pltpu.make_async_copy(conv_ref, conv_all.at[dp], own_sem)
    own.start()
    cot_in.start()
    rows_all[grp] = wave_ref[...]
    first_all[dp] = first_ref[...]
    cot_wide[255] = jnp.zeros((4, 512), BF16)
    even_rows[256:264] = jnp.zeros((8, 512), F32)
    acc[...] = jnp.zeros_like(acc)
    pl.semaphore_wait(barrier, 11)

    for j in range(1, 8):
        send(first_ref, first_all.at[dp], first_ss.at[j], first_rs.at[dp], ((dp + j) % 8, grp))
    for j in range(1, 4):
        send(wave_ref, rows_all.at[grp], row_ss.at[j], row_rs.at[grp], (dp, (grp + j) % 4))
    mine = conv_ref.at[grp]
    for j in (2, 1, 3):
        send(mine, conv_all.at[dp, grp], own_ss.at[j], conv_rs.at[dp, grp], (zpeer(j), grp))
    send(mine, conv_all.at[dp, grp], own_ss.at[0], conv_rs.at[dp, grp], ypeer)

    def pass_quarter(p, k, to_y):
        piece = conv_all.at[p, grp]
        arrived(piece, own_ss.at[0], conv_rs.at[p, grp], xpeer)
        send(piece, piece, xfw_ss.at[k], conv_rs.at[p, grp], xpeer)
        if to_y:
            send(piece, piece, yfw_ss.at[k], conv_rs.at[p, grp], ypeer)
        send(piece, piece, cfw_ss.at[k], conv_rs.at[p, grp], partner)

    def pass_across(p, k):
        q = (1 - xpos) * 2 + core
        piece = conv_all.at[p, q]
        arrived(piece, own_ss.at[0], conv_rs.at[p, q], xpeer)
        send(piece, piece, cfw_ss.at[8 + k], conv_rs.at[p, q], partner)

    def column(j):
        return ((zpos + j) % 4) * 2 + 1 - ypos

    cot_in.wait()

    def split_rows(i, _):
        part = pl.ds(pl.multiple_of(i * CHUNK, CHUNK), CHUNK)
        block = cot_wide[part].astype(F32)
        for r in range(4):
            cot_rows[r, part] = block[:, r, :].astype(BF16)
        return 0

    lax.fori_loop(0, 256 // CHUNK, split_rows, 0)

    pass_quarter(column(0), 0, False)
    for j in (1, 3):
        pass_quarter(zpeer(j), j, True)

    for j in range(1, 4):
        p = (grp + j) % 4
        arrived(rows_all.at[p], row_ss.at[j], row_rs.at[p], (dp, p))

    row_ids = lax.broadcasted_iota(jnp.int32, (16, 256), 0)
    pair_ids = lax.broadcasted_iota(jnp.int32, (16, 256), 1).astype(F32) * 2.0
    for r in range(4):
        place = (grp * 4 + r).astype(F32)
        chosen = jnp.zeros((16, 256), F32)
        for s in range(4):
            for i in range(4):
                row = rows_all[s, i].astype(F32)
                chosen = chosen + row * (row[10:11] == place).astype(F32)
        length = chosen[11:12] * 16.0 + chosen[12:13]
        count = jnp.floor((length - 9.5) * 0.2) + 1.0
        counts[r] = jnp.concatenate([count, count], axis=1)
        one = jnp.where(row_ids == 10, 1.0, 0.0)
        even = jnp.where(row_ids < 10, chosen, one)
        following = pltpu.roll(pltpu.roll(chosen, 255, 1), 5, 0)
        odd = jnp.where(row_ids < 5, pltpu.roll(chosen, 11, 0), jnp.where(row_ids < 10, following, one))
        even = jnp.where(pair_ids < count, even, 0.0).astype(BF16)
        odd = jnp.where(pair_ids + 1.0 < count, odd, 0.0).astype(BF16)
        for k in range(3):
            lhs_even[r, 16 * k : 16 * k + 16] = even
            lhs_odd[r, 16 * k : 16 * k + 16] = odd
        inner = (((1,), (1,)), ((), ()))
        gram[r] = lax.dot_general(even, even, inner, preferred_element_type=F32) + lax.dot_general(
            odd, odd, inner, preferred_element_type=F32
        )

    pass_quarter(zpeer(2), 2, True)

    for j in range(1, 8):
        p = (dp + j) % 8
        arrived(first_all.at[p], first_ss.at[j], first_rs.at[p], (p, grp))
    for b in range(4):
        first16[:, b * 128 : b * 128 + 128] = first_all[2 * b] + first_all[2 * b + 1]

    def front(r, _):
        weights = first16[...].astype(F32)
        gain, bias = gain_ref[...], bias_ref[...]
        inv_count = 1.0 / counts[r]
        tap_sums = gram[r][:, 10:11]
        mean = jnp.sum(weights * tap_sums, axis=0, keepdims=True) * inv_count
        means[r] = mean
        centre = gram[r] - tap_sums * gram[r][10:11, :] * inv_count[:, 0:16]
        high = centre.astype(BF16)
        rest = centre - high.astype(F32)
        middle_part = rest.astype(BF16)
        low = (rest - middle_part.astype(F32)).astype(BF16)
        taps16 = first16[...]
        cross[r] = (
            jnp.dot(high, taps16, preferred_element_type=F32)
            + jnp.dot(middle_part, taps16, preferred_element_type=F32)
        ) + jnp.dot(low, taps16, preferred_element_type=F32)
        ids = lax.broadcasted_iota(jnp.int32, (16, 512), 0)
        three_parts(jnp.where(ids == 10, -mean, weights), rhs)
        turn = (((0,), (0,)), ((), ()))
        total = jnp.zeros((8, 512), F32)
        for lhs in (lhs_even, lhs_odd):
            centred = lax.dot_general(lhs[r], rhs[...], turn, preferred_element_type=F32)
            total = total + fold_rows(centred * centred)
        inv = lax.rsqrt(jnp.sum(total, axis=0, keepdims=True) * inv_count + 1e-05)
        inv_all[r] = inv
        factor = inv * gain
        three_parts(jnp.where(ids == 10, bias - mean * factor, weights * factor), rhs)
        for half, lhs in enumerate((lhs_even, lhs_odd)):
            shifted = lax.dot_general(lhs[r], rhs[...], turn, preferred_element_type=F32)
            for i in range(256 // CHUNK):
                value = shifted[i * CHUNK : (i + 1) * CHUNK]
                phi, grad = phi_and_slope(value)
                hidden = value * phi
                rows = pl.ds(pl.multiple_of(r * 256 + i * CHUNK, CHUNK), CHUNK)
                slope[rows, half * 512 : half * 512 + 512] = grad.astype(BF16)
                taps[rows, half * 512 : half * 512 + 512] = hidden.astype(BF16)
                if half == 0:
                    even_rows[i * CHUNK : (i + 1) * CHUNK] = hidden
        all_rows = pl.ds(pl.multiple_of(r * 256, 256), 256)
        taps[all_rows, 1024:1536] = even_rows[1:257].astype(BF16)
        return 0

    lax.fori_loop(0, 1, front, 0)
    for j in (1, 3):
        pass_quarter(column(j), 3 + j, False)
    pass_across(column(0), 0)
    lax.fori_loop(1, 2, front, 0)
    pass_quarter(column(2), 5, False)
    for j in (1, 3):
        pass_across(zpeer(j), j)
    lax.fori_loop(2, 3, front, 0)
    pass_across(zpeer(2), 2)
    for j in (1, 3):
        pass_across(column(j), 3 + j)
    lax.fori_loop(3, 4, front, 0)
    pass_across(column(2), 5)
    own.wait()
    for j in range(1, 8):
        p = (dp + j) % 8
        for q in (xpos * 2 + 1 - core, (1 - xpos) * 2 + 1 - core):
            arrived(conv_all.at[p, q], own_ss.at[0], conv_rs.at[p, q], partner)

    def turn_weights(k, _):
        part = pl.ds(pl.multiple_of(k * 128, 128), 128)
        turned[:, part] = conv_all[pl.ds(k * 2, 2)].reshape(128, 1536).T
        return 0

    for k in range(4):
        turned[:, k * 128 : k * 128 + 128] = conv_all[2 * k : 2 * k + 2].reshape(128, 1536).T

    even_rows[0:8] = jnp.zeros((8, 512), F32)

    def middle(r, _):
        all_rows = pl.ds(pl.multiple_of(r * 256, 256), 256)
        second = jnp.dot(taps[all_rows, :], turned[...], preferred_element_type=F32)
        count2 = jnp.floor((counts[r] - 2.5) * 0.5) + 1.0
        ids = lax.broadcasted_iota(jnp.int32, (CHUNK, 512), 0).astype(F32)
        for i in range(256 // CHUNK):
            valid = ids + float(i * CHUNK) < count2
            value = second[i * CHUNK : (i + 1) * CHUNK]
            phi, grad = phi_and_slope(value)
            part = slice(i * CHUNK, (i + 1) * CHUNK)
            feat_rows[r, part] = jnp.where(valid, value * phi, 0.0).astype(BF16)
            rows = pl.ds(pl.multiple_of(r * 256 + i * CHUNK, CHUNK), CHUNK)
            back = jnp.where(valid, cot_rows[r, part].astype(F32) * grad, 0.0)
            delta[rows, :] = back.astype(BF16)
            even_rows[8 + i * CHUNK : 8 + (i + 1) * CHUNK] = back
        before[all_rows, :] = even_rows[7:263].astype(BF16)
        delta_turned[:, all_rows] = delta[all_rows, :].T
        return 0

    lax.fori_loop(0, 4, middle, 0)

    stage = {}

    def weight_grad(b):
        first, width = BLOCKS[b]
        cols = slice(first, first + width)
        part = jnp.dot(delta_turned[...], taps[:, cols], preferred_element_type=F32)
        part = part.reshape(8, 2, 2, 16, width)
        gc_full[:, :, :, :, cols] = part
        gc_send[:, :, :, :, cols] = part.astype(BF16)
        stage[b] = remote(
            gc_send.at[:, :, 1 - core, :, cols], gc_r1.at[:, :, :, cols], s1_ss.at[b], s1_rs.at[b], partner
        )
        stage[b].start()

    def reduce_core(b):
        first, width = BLOCKS[b]
        cols = slice(first, first + width)
        stage[b].wait()
        for j in range(4):
            x_at = xpos if j % 2 == 0 else 1 - xpos
            y_at = ypos if j // 2 == 0 else 1 - ypos
            for z in range(4):
                d = z * 2 + y_at
                total = gc_full[d, x_at, core, :, cols] + gc_r1[d, x_at, :, cols].astype(F32)
                if j == 0:
                    gc_k2[z, :, cols] = total
                else:
                    gc_s2[j, z, :, cols] = total.astype(BF16)
            if j > 0:
                send(
                    gc_s2.at[j, :, :, cols], gc_r2.at[j, :, :, cols], s2_ss.at[b, j], s2_rs.at[b, j], plane[j]
                )

    def reduce_plane(b):
        first, width = BLOCKS[b]
        cols = slice(first, first + width)
        for j in range(1, 4):
            arrived(gc_r2.at[j, :, :, cols], s2_ss.at[b, j], s2_rs.at[b, j], plane[j])
        for z in range(4):
            total = gc_k2[z, :, cols]
            for j in range(1, 4):
                total = total + gc_r2[j, z, :, cols].astype(F32)
            gc_k3[z, :, cols] = total
            gc_s3[z, :, cols] = total.astype(BF16)
        for j in (2, 1, 3):
            zp = (zpos + j) % 4
            send(
                gc_s3.at[zp, :, cols], gc_r3.at[zpos, :, cols], s3_ss.at[b, j], s3_rs.at[b, zpos], (zp * 2 + ypos, grp)
            )

    def reduce_line(b):
        first, width = BLOCKS[b]
        cols = slice(first, first + width)
        total = gc_k3[zpos, :, cols]
        for j in range(1, 4):
            zp = (zpos + j) % 4
            arrived(gc_r3.at[zp, :, cols], s3_ss.at[b, j], s3_rs.at[b, zp], (zp * 2 + ypos, grp))
            total = total + gc_r3[zp, :, cols].astype(F32)
        gc_out[grp, :, cols] = total.astype(BF16)
        for j in range(1, 4):
            piece = gc_out.at[grp, :, cols]
            send(piece, piece, s4_ss.at[b, j], s4_rs.at[b, grp], (dp, (grp + j) % 4))

    def gathered(b):
        first, width = BLOCKS[b]
        cols = slice(first, first + width)
        for j in range(1, 4):
            p = (grp + j) % 4
            arrived(gc_out.at[p, :, cols], s4_ss.at[b, j], s4_rs.at[b, p], (dp, p))
        gconv_ref[:, cols] = gc_out[:, :, cols].astype(F32).reshape(64, width)

    def backward(r, _):
        rows = pl.ds(pl.multiple_of(r * 256, 256), 256)
        weights = conv_all[...].reshape(512, 1536)
        even = jnp.dot(delta[rows, :], weights[:, 0:512], preferred_element_type=F32) + jnp.dot(
            before[rows, :], weights[:, 1024:1536], preferred_element_type=F32
        )
        odd = jnp.dot(delta[rows, :], weights[:, 512:1024], preferred_element_type=F32)
        even = (even * slope[rows, 0:512].astype(F32)).astype(BF16)
        odd = (odd * slope[rows, 512:1024].astype(F32)).astype(BF16)
        found = jnp.dot(lhs_even[r, 0:16], even, preferred_element_type=F32) + jnp.dot(
            lhs_odd[r, 0:16], odd, preferred_element_type=F32
        )
        inv_count, inv, mean = 1.0 / counts[r], inv_all[r], means[r]
        plain = found[10:11]
        with_normed = inv * (
            jnp.sum(first16[...].astype(F32) * found, axis=0, keepdims=True) - mean * plain
        )
        tap_sums = gram[r][:, 10:11]
        grads = (inv * gain_ref[...]) * (
            found - tap_sums * (plain * inv_count) - cross[r] * (with_normed * inv * inv_count)
        )
        ids = lax.broadcasted_iota(jnp.int32, (16, 512), 0)
        grads = jnp.where(ids == 10, with_normed, jnp.where(ids == 11, plain, grads))
        acc[...] += grads
        return 0

    for b in range(len(BLOCKS)):
        weight_grad(b)
        if b > 0:
            reduce_core(b - 1)
    lax.fori_loop(0, 1, backward, 0)
    reduce_core(len(BLOCKS) - 1)
    lax.fori_loop(1, 4, backward, 0)

    total = acc[...]
    sm_half[0] = total[:, 0:256]
    sm_half[1] = total[:, 256:512]
    small = remote(sm_half.at[1 - core], sm_core, sc_ss, sc_rs, partner)
    small.start()
    reduce_plane(0)
    small.wait()
    here = xpos * 2 + ypos
    sm_xy[here] = sm_half[core] + sm_core[...]
    for j in range(1, 4):
        send(sm_xy.at[here], sm_xy.at[here], sxy_ss.at[j], sxy_rs.at[j], plane[j])
    reduce_plane(1)

    def join_rows(i, _):
        part = pl.ds(pl.multiple_of(i * CHUNK, CHUNK), CHUNK)
        parts = [feat_rows[r, part].astype(F32) for r in range(4)]
        feat_wide[part] = jnp.stack(parts, axis=1).astype(BF16)
        return 0

    lax.fori_loop(0, 256 // CHUNK, join_rows, 0)
    feat_out = pltpu.make_async_copy(feat_wide.at[0:255], feat_ref, feat_sem)
    feat_out.start()
    there = ((1 - xpos) * 2 + ypos, xpos * 2 + 1 - ypos, (1 - xpos) * 2 + 1 - ypos)
    for j in range(1, 4):
        arrived(sm_xy.at[there[j - 1]], sxy_ss.at[j], sxy_rs.at[j], plane[j])
    sm_z[zpos] = (sm_xy[0] + sm_xy[1]) + (sm_xy[2] + sm_xy[3])
    for j in (2, 1, 3):
        zp = (zpos + j) % 4
        send(sm_z.at[zpos], sm_z.at[zpos], sz_ss.at[j], sz_rs.at[zpos], (zp * 2 + ypos, grp))
    reduce_plane(2)
    for b in range(len(BLOCKS)):
        reduce_line(b)
    for j in range(1, 4):
        zp = (zpos + j) % 4
        arrived(sm_z.at[zp], sz_ss.at[j], sz_rs.at[zp], (zp * 2 + ypos, grp))
    sm_out[core] = (sm_z[0] + sm_z[1]) + (sm_z[2] + sm_z[3])
    last = remote(sm_out.at[core], sm_out.at[core], so_ss, so_rs.at[core], partner)
    last.start()
    for b in range(len(BLOCKS)):
        gathered(b)
    arrived(sm_out.at[1 - core], so_ss, so_rs.at[1 - core], partner)
    small_sum = jnp.concatenate([sm_out[0], sm_out[1]], axis=1)
    ggain_ref[...] = small_sum[10:11]
    gbias_ref[...] = small_sum[11:12]
    gfirst_ref[...] = pltpu.roll(small_sum, (8 - dp) % 8 * 64, 1)[0:10, 0:64]
    feat_out.wait()
    last.wait_send()
    for c in sends:
        c.wait_send()


def pass_on(*refs):
    sources, targets, buffers, (in_sem, out_sem) = refs[0:5], refs[5:10], refs[10:15], refs[15:17]
    spans = [(0, pl.ds(0, 64)), (0, pl.ds(64, 64)), (0, pl.ds(128, 64)), (0, pl.ds(192, 63))]
    views = [tuple(group[k].at[span] for group in (sources, buffers, targets)) for k, span in spans]
    views += [(sources[k], buffers[k], targets[k]) for k in range(1, 5)]
    reads, writes = [], []
    for k, (source, buffer, target) in enumerate(views):
        c = pltpu.make_async_copy(source, buffer, in_sem.at[k])
        c.start()
        reads.append(c)
    for k, (source, buffer, target) in enumerate(views):
        reads[k].wait()
        c = pltpu.make_async_copy(buffer, target, out_sem.at[k])
        c.start()
        writes.append(c)
    for c in writes:
        c.wait()


def local_fused(
    waveform, lengths, packing, first_weight, norm_gain, norm_bias, conv_weight, grad_features
):
    dp = lax.axis_index("dp")
    blocks = waveform.reshape(4, 256, 10).transpose(0, 2, 1)
    notes = jnp.stack([packing, lengths // 16, lengths % 16], axis=1).astype(BF16)
    notes = jnp.broadcast_to(notes[:, :, None], (4, 3, 256))
    wave_rows = jnp.concatenate([blocks, notes, jnp.zeros((4, 3, 256), BF16)], axis=1)
    stacked = jnp.concatenate([first_weight.T, jnp.zeros((6, 64), BF16)], axis=0)
    odd_half = dp % 2 == 1
    blank = jnp.zeros_like(stacked)
    first_rows = jnp.concatenate(
        [jnp.where(odd_half, blank, stacked), jnp.where(odd_half, stacked, blank)], axis=1
    )
    vmem = lambda *shape: pltpu.VMEM(shape, F32)
    vmem16 = lambda *shape: pltpu.VMEM(shape, BF16)
    dma = pltpu.SemaphoreType.DMA
    n = len(BLOCKS)
    features, grad_conv, grad_first, grad_gain, grad_bias = pl.pallas_call(
        fused_kernel,
        out_shape=(
            jax.ShapeDtypeStruct((255, 4, 512), BF16),
            jax.ShapeDtypeStruct((64, 1536), F32),
            jax.ShapeDtypeStruct((10, 64), F32),
            jax.ShapeDtypeStruct((1, 512), F32),
            jax.ShapeDtypeStruct((1, 512), F32),
        ),
        in_specs=[pl.BlockSpec(memory_space=pltpu.VMEM)] * 2
        + [pl.BlockSpec(memory_space=pl.ANY)]
        + [pl.BlockSpec(memory_space=pltpu.VMEM)] * 2
        + [pl.BlockSpec(memory_space=pl.ANY)],
        out_specs=[pl.BlockSpec(memory_space=pl.ANY)] + [pl.BlockSpec(memory_space=pltpu.VMEM)] * 4,
        scratch_shapes=[
            vmem16(4, 4, 16, 256), vmem16(8, 16, 128), vmem16(16, 512), vmem16(8, 4, 16, 1536), vmem16(1536, 512),
            vmem16(1024, 1024), vmem16(1024, 1536), vmem(264, 512), vmem16(1024, 512), vmem16(1024, 512),
            vmem16(512, 1024),
            vmem16(256, 4, 512), vmem16(4, 256, 512), vmem16(256, 4, 512), vmem16(4, 256, 512),
            vmem16(4, 48, 256), vmem16(4, 48, 256), vmem16(48, 512), vmem(4, 1, 512), vmem(4, 1, 512),
            vmem(4, 1, 512), vmem(4, 16, 16), vmem(4, 16, 512), vmem(16, 512),
            vmem(8, 2, 2, 16, 1536), vmem16(8, 2, 2, 16, 1536), vmem16(8, 2, 16, 1536),
            vmem(4, 16, 1536), vmem16(4, 4, 16, 1536), vmem16(4, 4, 16, 1536),
            vmem(4, 16, 1536), vmem16(4, 16, 1536), vmem16(4, 16, 1536), vmem16(4, 16, 1536),
            vmem(2, 16, 256), vmem(16, 256), vmem(4, 16, 256), vmem(4, 16, 256), vmem(2, 16, 256),
            dma((4,)), dma((4,)), dma((8,)), dma((8,)), dma((4,)), dma((4,)), dma((8,)), dma((16,)), dma((8, 4)),
            dma, dma, dma,
            dma((n,)), dma((n,)), dma((n, 4)), dma((n, 4)), dma((n, 4)), dma((n, 4)), dma((n, 4)), dma((n, 4)),
            dma, dma, dma((4,)), dma((4,)), dma((4,)), dma((4,)), dma, dma((2,)),
        ],
        compiler_params=pltpu.CompilerParams(
            collective_id=0, has_side_effects=True, vmem_limit_bytes=60 * 1024 * 1024
        ),
    )(wave_rows, first_rows, conv_weight.reshape(4, 16, 1536), norm_gain[None], norm_bias[None], grad_features.transpose(1, 0, 2))
    results = (features, grad_conv, grad_first, grad_gain, grad_bias)
    features, grad_conv, grad_first, grad_gain, grad_bias = pl.pallas_call(
        pass_on,
        out_shape=tuple(jax.ShapeDtypeStruct(each.shape, each.dtype) for each in results),
        in_specs=[pl.BlockSpec(memory_space=pl.ANY)] * 5,
        out_specs=[pl.BlockSpec(memory_space=pl.ANY)] * 5,
        scratch_shapes=[pltpu.VMEM(each.shape, each.dtype) for each in results] + [dma((8,)), dma((8,))],
    )(*results)
    return (features.transpose(1, 0, 2), grad_conv, grad_first.T, grad_gain[0], grad_bias[0])


def solution(mesh):
    shape = dict(mesh.shape)
    fused = shape["dp"] == 8 and shape["group"] == 4
    return jax.shard_map(
        local_fused if fused else local,
        mesh=mesh,
        in_specs=(
            P(("dp", "group"), None),
            P(("dp", "group")),
            P(("dp", "group")),
            P("dp", None),
            P(),
            P(),
            P("dp", None),
            P(("dp", "group"), None, None),
        ),
        out_specs=(P(("dp", "group"), None, None), P("dp", None), P("dp", None), P(), P()),
        check_vma=False,
    )
```

```python
import functools

import jax
import jax.numpy as jnp
from jax import lax
from jax.experimental import pallas as pl
from jax.experimental.pallas import tpu as pltpu
from jax.sharding import PartitionSpec as P

MESH = pl.DeviceIdType.MESH
F32, BF16 = jnp.float32, jnp.bfloat16
CHUNK = 32


def gelu_slope(values):
    return (
        0.5 * (1.0 + lax.erf(values * 0.7071067811865476))
        + values * jnp.exp(-0.5 * values * values) * 0.3989422804014327
    )


def tap_matrix(hidden, frames_second):
    row_count, frames_first, channels = hidden.shape
    zero_frame = jnp.zeros((row_count, 1, channels), hidden.dtype)
    paired = jnp.concatenate([hidden, zero_frame], axis=1).reshape(
        row_count, frames_second + 1, 2, channels
    )
    even_half = paired[:, :, 0]
    odd_half = paired[:, :, 1]
    stacked = jnp.concatenate(
        [even_half[:, :frames_second], odd_half[:, :frames_second], even_half[:, 1:]], axis=2
    )
    return stacked.reshape(row_count * frames_second, 3 * channels)


def spread_back(back_taps, row_count, frames_second, frames_first):
    first_tap = back_taps[0].reshape(row_count, frames_second, -1)
    middle_tap = back_taps[1].reshape(row_count, frames_second, -1)
    last_tap = back_taps[2].reshape(row_count, frames_second, -1)
    channels = first_tap.shape[2]
    zero_frame = jnp.zeros((row_count, 1, channels), jnp.float32)
    even_half = jnp.concatenate([first_tap, zero_frame], axis=1) + jnp.concatenate(
        [zero_frame, last_tap], axis=1
    )
    odd_half = jnp.concatenate([middle_tap, zero_frame], axis=1)
    joined = jnp.stack([even_half, odd_half], axis=2).reshape(
        row_count, 2 * frames_second + 2, channels
    )
    return joined[:, :frames_first]


def local(
    waveform, lengths, packing, first_weight, norm_gain, norm_bias, conv_weight, grad_features
):
    row_count, capacity = waveform.shape
    channels = norm_gain.shape[0]
    frames_first = capacity // 5 - 1
    frames_second = (capacity // 5 - 2) // 2
    groups = lax.axis_size("group")
    own_group = lax.axis_index("group")
    group_rows = groups * row_count
    all_pack, all_lengths = (
        lax.all_gather(packing, "group", axis=0, tiled=True),
        lax.all_gather(lengths, "group", axis=0, tiled=True),
    )
    target = all_pack // row_count
    slot_index = all_pack % row_count
    positions = jnp.arange(group_rows)
    source = positions // row_count
    same_source = source[:, None] == source[None, :]
    same_target = target[:, None] == target[None, :]
    before = positions[:, None] > positions[None, :]
    rank_among = jnp.sum((same_source & same_target & before).astype(jnp.int32), axis=1)
    arriving = target == own_group
    slot_ids = jnp.arange(row_count)
    choose_slot = (slot_index[None, :] == slot_ids[:, None]) & arriving[None, :]
    local_lengths = jnp.sum(jnp.where(choose_slot, all_lengths[None, :], 0), axis=1)
    per_peer = 2 * ((row_count + 2 * groups - 1) // (2 * groups))
    lane_ids = jnp.arange(per_peer)
    own_target = lax.dynamic_slice_in_dim(target, own_group * row_count, row_count)
    own_rank = lax.dynamic_slice_in_dim(rank_among, own_group * row_count, row_count)
    outgoing = (
        (own_target[None, None, :] == jnp.arange(groups)[:, None, None])
        & (own_rank[None, None, :] == lane_ids[None, :, None])
    ).astype(jnp.bfloat16)
    send_rows = jnp.einsum(
        "gkr,rs->gks", outgoing, waveform, preferred_element_type=jnp.float32
    ).astype(jnp.bfloat16)
    received = lax.all_to_all(send_rows, "group", split_axis=0, concat_axis=0, tiled=True)
    pick_slots = (
        choose_slot[:, :, None] & (rank_among[None, :, None] == lane_ids[None, None, :])
    ).astype(jnp.float32)
    pick_slots = jnp.sum(pick_slots.reshape(row_count, groups, row_count, per_peer), axis=2).astype(
        jnp.bfloat16
    )
    wave_rows = jnp.einsum(
        "lsk,skn->ln", pick_slots, received, preferred_element_type=jnp.float32
    ).astype(jnp.bfloat16)
    first_whole = lax.all_gather(first_weight, "dp", axis=0, tiled=True)
    in_length = jnp.arange(capacity)[None, :] < local_lengths[:, None]
    masked = jnp.where(in_length, wave_rows, jnp.zeros_like(wave_rows))
    blocks = masked.reshape(row_count, capacity // 5, 5)
    taps_first = jnp.concatenate([blocks[:, :-1], blocks[:, 1:]], axis=2).reshape(
        row_count * frames_first, 10
    )
    conv_first = lax.dot_general(
        taps_first, first_whole, (((1,), (1,)), ((), ())), preferred_element_type=jnp.float32
    )
    conv_first = conv_first.reshape(row_count, frames_first, channels)
    count_first = (local_lengths - 10) // 5 + 1
    count_second = (count_first - 3) // 2 + 1
    valid_first = (jnp.arange(frames_first)[None, :] < count_first[:, None]).astype(jnp.float32)[
        :, :, None
    ]
    valid_second = (jnp.arange(frames_second)[None, :] < count_second[:, None]).astype(jnp.float32)[
        :, :, None
    ]
    count_float = count_first.astype(jnp.float32)[:, None, None]
    row_mean = jnp.sum(conv_first * valid_first, axis=1, keepdims=True) / count_float
    centred = (conv_first - row_mean) * valid_first
    row_var = jnp.sum(centred * centred, axis=1, keepdims=True) / count_float
    inv_scale = lax.rsqrt(row_var + 1e-05)
    normed = (conv_first - row_mean) * inv_scale
    shifted = normed * norm_gain + norm_bias
    hidden = (jax.nn.gelu(shifted, approximate=False) * valid_first).astype(jnp.bfloat16)
    taps_second = tap_matrix(hidden, frames_second)
    conv_whole = lax.all_gather(conv_weight, "dp", axis=0, tiled=True)
    conv_second = lax.dot_general(
        taps_second, conv_whole, (((1,), (1,)), ((), ())), preferred_element_type=jnp.float32
    )
    conv_second = conv_second.reshape(row_count, frames_second, channels)
    features = (jax.nn.gelu(conv_second, approximate=False) * valid_second).astype(jnp.bfloat16)
    delta_second = (
        grad_features.astype(jnp.float32) * valid_second * gelu_slope(conv_second)
    ).astype(jnp.bfloat16)
    delta_flat = delta_second.reshape(row_count * frames_second, channels)
    back_taps = tuple(
        (
            jnp.dot(
                delta_flat,
                conv_whole[:, tap_index * channels : (tap_index + 1) * channels],
                preferred_element_type=jnp.float32,
            )
            for tap_index in range(3)
        )
    )
    share = lax.psum_scatter(
        lax.dot_general(
            delta_flat, taps_second, (((0,), (0,)), ((), ())), preferred_element_type=jnp.float32
        ),
        "dp",
        scatter_dimension=0,
        tiled=True,
    )
    grad_conv = lax.psum(share, "group")
    delta_hidden = spread_back(back_taps, row_count, frames_second, frames_first)
    delta_norm = delta_hidden * valid_first * gelu_slope(shifted)
    gain_term = jnp.sum(delta_norm * normed, axis=(0, 1))
    bias_term = jnp.sum(delta_norm, axis=(0, 1))
    scaled = delta_norm * norm_gain
    mean_grad = jnp.sum(scaled, axis=1, keepdims=True) / count_float
    mean_cross = jnp.sum(scaled * normed, axis=1, keepdims=True) / count_float
    delta_first = ((scaled - mean_grad - normed * mean_cross) * inv_scale * valid_first).astype(
        jnp.bfloat16
    )
    first_term = lax.dot_general(
        delta_first.reshape(row_count * frames_first, channels),
        taps_first,
        (((0,), (0,)), ((), ())),
        preferred_element_type=jnp.float32,
    )
    stacked = jnp.concatenate([first_term, gain_term[:, None], bias_term[:, None]], axis=1)
    summed = lax.psum(stacked, ("dp", "group"))
    shard_rows = channels // lax.axis_size("dp")
    grad_first = lax.dynamic_slice_in_dim(
        summed[:, :10], lax.axis_index("dp") * shard_rows, shard_rows, 0
    )
    return (features, grad_conv, grad_first, summed[:, 10], summed[:, 11])


BLOCKS = ((0, 512), (512, 512), (1024, 512))


def phi_and_slope(values):
    phi = 0.5 + 0.5 * lax.erf(values * 0.7071067811865476)
    return phi, phi + (values * 0.3989422804014327) * jnp.exp2(values * values * -0.7213475204444817)


def fold_rows(block):
    return jnp.sum(block.reshape(block.shape[0] // 8, 8, block.shape[1]), axis=0)


def three_parts(values, out):
    high = values.astype(BF16)
    rest = values - high.astype(F32)
    middle = rest.astype(BF16)
    out[0:16] = high
    out[16:32] = middle
    out[32:48] = (rest - middle.astype(F32)).astype(BF16)


def fused_kernel(
    wave_in, lengths_in, packing_in, first_in, conv_ref, gain_in, bias_in, cot_ref,
    feat_ref, gconv_ref, gfirst_ref, ggain_ref, gbias_ref,
    wave_own, lengths_own, packing_own, first_own, gain_ref, bias_ref, wide, narrow, wave_ref, first_ref, second, in_sem,
    rows_all, first_all, first16, conv_all, turned, slope, taps, even_rows, delta, before, delta_turned,
    cot_wide, cot_rows, feat_wide, feat_rows, lhs_even, lhs_odd, rhs, counts, means, inv_all, gram, cross, acc,
    gc_full, gc_send, gc_r1, gc_k2, gc_s2, gc_r2, gc_k3, gc_s3, gc_r3, gc_out,
    sm_half, sm_core, sm_xy, sm_z, sm_out,
    row_ss, row_rs, first_ss, first_rs, own_ss, fw_ss, conv_rs, own_sem, cot_sem, feat_sem,
    s1_ss, s1_rs, s2_ss, s2_rs, s3_ss, s3_rs, s4_ss, s4_rs,
    sc_ss, sc_rs, sxy_ss, sxy_rs, sz_ss, sz_rs, so_ss, so_rs,
):
    dp, grp = lax.axis_index("dp"), lax.axis_index("group")
    core, xpos = grp % 2, grp // 2
    ypos, zpos = dp % 2, dp // 2
    partner = (dp, xpos * 2 + (1 - core))
    xpeer = (dp, (1 - xpos) * 2 + core)
    ypeer = (zpos * 2 + (1 - ypos), grp)
    corner = (zpos * 2 + (1 - ypos), (1 - xpos) * 2 + core)
    plane = (None, xpeer, ypeer, corner)

    lines = (zpos, zpos + 1 - 2 * (zpos % 2), (zpos + 2) % 4, 3 - zpos)
    near = zpos // 2
    far = 1 - near

    def zpeer(j):
        return lines[j] * 2 + ypos

    def remote(src, dst, ss, rs, dev):
        return pltpu.make_async_remote_copy(
            src_ref=src, dst_ref=dst, send_sem=ss, recv_sem=rs, device_id=dev, device_id_type=MESH
        )

    sends = []

    def send(src, dst, ss, rs, dev):
        c = remote(src, dst, ss, rs, dev)
        c.start()
        sends.append(c)

    def arrived(ref, ss, rs, dev):
        remote(ref, ref, ss, rs, dev).wait_recv()

    cot_in = pltpu.make_async_copy(cot_ref, cot_wide.at[0:255], cot_sem)
    barrier = pltpu.get_barrier_semaphore()
    for j in (3, 2, 1):
        for y_at in (1 - ypos, ypos):
            pl.semaphore_signal(barrier, inc=1, device_id=(lines[j] * 2 + y_at, grp), device_id_type=MESH)
    for device in (corner, ypeer, xpeer, partner, (dp, (1 - xpos) * 2 + 1 - core)):
        pl.semaphore_signal(barrier, inc=1, device_id=device, device_id_type=MESH)
    own = pltpu.make_async_copy(conv_ref, conv_all.at[dp], own_sem)
    own.start()
    loads = []
    pairs = (
        (wave_in, wave_own), (first_in, first_own), (lengths_in, lengths_own), (packing_in, packing_own),
        (gain_in, gain_ref), (bias_in, bias_ref),
    )
    for k, (source, target) in enumerate(pairs):
        c = pltpu.make_async_copy(source, target, in_sem.at[k])
        c.start()
        loads.append(c)
    cot_in.start()
    cot_wide[255] = jnp.zeros((4, 512), BF16)
    even_rows[256:264] = jnp.zeros((8, 512), F32)
    acc[...] = jnp.zeros_like(acc)
    for c in loads:
        c.wait()
    piece = first_own[...].astype(F32)
    piece = jnp.concatenate([piece, jnp.zeros((6, 64), F32)], axis=0)
    piece = jnp.concatenate([piece, piece], axis=1)
    lane = lax.broadcasted_iota(jnp.int32, (16, 128), 1)
    piece = jnp.where(lane // 64 == dp % 2, piece, 0.0).astype(BF16)
    first_ref[...] = piece
    first_all[dp] = piece
    wave = wave_own[...].astype(F32)
    wave = jnp.concatenate([wave, wave], axis=0)
    wide[...] = jnp.concatenate([wave] * 16, axis=0).T
    lane = lax.broadcasted_iota(jnp.int32, (256, 128), 1) // 4
    taken = jnp.zeros((256, 128), F32)
    for k in range(10):
        taken = jnp.where(lane == k, wide[pl.ds(k, 256, stride=10), :], taken)
    narrow[0] = taken[0:128].T
    narrow[1] = taken[128:256].T
    row_ids = lax.broadcasted_iota(jnp.int32, (16, 256), 0)
    for r in range(4):
        place = packing_own[0:1, r : r + 1]
        length = lengths_own[0:1, r : r + 1]
        notes = jnp.where(row_ids == 10, place, jnp.where(row_ids == 11, length // 16, length % 16)).astype(F32)
        block = jnp.concatenate([narrow[0, pl.ds(r, 16, stride=4), :], narrow[1, pl.ds(r, 16, stride=4), :]], axis=1)
        block = jnp.where(row_ids < 10, block, notes).astype(BF16)
        wave_ref[r] = block
        rows_all[grp, r] = block
    pl.semaphore_wait(barrier, 11)

    for j in (3, 2, 1, 0):
        for y_at in (1 - ypos, ypos) if j > 0 else (1 - ypos,):
            peer = (lines[j] * 2 + y_at, grp)
            send(first_ref, first_all.at[dp], first_ss.at[2 * j + (0 if y_at is ypos else 1)], first_rs.at[dp], peer)
    for j in range(1, 4):
        send(wave_ref, rows_all.at[grp], row_ss.at[j], row_rs.at[grp], (dp, (grp + j) % 4))
    mine = conv_ref.at[grp]
    across = (1 - xpos) * 2 + core
    send(mine, conv_all.at[dp, grp], own_ss.at[0], conv_rs.at[dp, grp], ypeer)
    send(mine, conv_all.at[dp, grp], own_ss.at[1], conv_rs.at[dp, grp], (zpeer(1), grp))
    send(conv_ref.at[across], conv_all.at[dp, across], own_ss.at[4], conv_rs.at[dp, across], (zpeer(1), grp))
    for j in (2, 3):
        send(mine, conv_all.at[dp, grp], own_ss.at[j], conv_rs.at[dp, grp], (zpeer(j), grp))
    passed = []

    def pass_on_piece(p, q, devices):
        piece = conv_all.at[p, q]
        arrived(piece, own_ss.at[0], conv_rs.at[p, q], xpeer)
        for device in devices:
            send(piece, piece, fw_ss.at[len(passed)], conv_rs.at[p, q], device)
            passed.append(device)

    def column(j):
        return lines[j] * 2 + 1 - ypos

    cot_in.wait()

    def split_rows(i, _):
        part = pl.ds(pl.multiple_of(i * CHUNK, CHUNK), CHUNK)
        block = cot_wide[part].astype(F32)
        for r in range(4):
            cot_rows[r, part] = block[:, r, :].astype(BF16)
        return 0

    lax.fori_loop(0, 256 // CHUNK, split_rows, 0)

    pass_on_piece(column(0), grp, (xpeer, partner))
    pass_on_piece(zpeer(1), grp, (ypeer, partner))

    for j in range(1, 4):
        p = (grp + j) % 4
        arrived(rows_all.at[p], row_ss.at[j], row_rs.at[p], (dp, p))

    pair_ids = lax.broadcasted_iota(jnp.int32, (16, 256), 1).astype(F32) * 2.0
    for r in range(4):
        place = (grp * 4 + r).astype(F32)
        chosen = jnp.zeros((16, 256), F32)
        for s in range(4):
            for i in range(4):
                row = rows_all[s, i].astype(F32)
                chosen = chosen + row * (row[10:11] == place).astype(F32)
        length = chosen[11:12] * 16.0 + chosen[12:13]
        count = jnp.floor((length - 9.5) * 0.2) + 1.0
        counts[r] = jnp.concatenate([count, count], axis=1)
        one = jnp.where(row_ids == 10, 1.0, 0.0)
        even = jnp.where(row_ids < 10, chosen, one)
        following = pltpu.roll(pltpu.roll(chosen, 255, 1), 5, 0)
        odd = jnp.where(row_ids < 5, pltpu.roll(chosen, 11, 0), jnp.where(row_ids < 10, following, one))
        even = jnp.where(pair_ids < count, even, 0.0).astype(BF16)
        odd = jnp.where(pair_ids + 1.0 < count, odd, 0.0).astype(BF16)
        for k in range(3):
            lhs_even[r, 16 * k : 16 * k + 16] = even
            lhs_odd[r, 16 * k : 16 * k + 16] = odd
        inner = (((1,), (1,)), ((), ()))
        gram[r] = lax.dot_general(even, even, inner, preferred_element_type=F32) + lax.dot_general(
            odd, odd, inner, preferred_element_type=F32
        )

    for j in range(1, 8):
        p = (dp + j) % 8
        arrived(first_all.at[p], first_ss.at[j], first_rs.at[p], (p, grp))
    for b in range(4):
        first16[:, b * 128 : b * 128 + 128] = first_all[2 * b] + first_all[2 * b + 1]

    def front(r, _):
        weights = first16[...].astype(F32)
        gain, bias = gain_ref[...], bias_ref[...]
        inv_count = 1.0 / counts[r]
        tap_sums = gram[r][:, 10:11]
        mean = jnp.sum(weights * tap_sums, axis=0, keepdims=True) * inv_count
        means[r] = mean
        centre = gram[r] - tap_sums * gram[r][10:11, :] * inv_count[:, 0:16]
        high = centre.astype(BF16)
        rest = centre - high.astype(F32)
        middle_part = rest.astype(BF16)
        low = (rest - middle_part.astype(F32)).astype(BF16)
        taps16 = first16[...]
        cross[r] = (
            jnp.dot(high, taps16, preferred_element_type=F32)
            + jnp.dot(middle_part, taps16, preferred_element_type=F32)
        ) + jnp.dot(low, taps16, preferred_element_type=F32)
        ids = lax.broadcasted_iota(jnp.int32, (16, 512), 0)
        three_parts(jnp.where(ids == 10, -mean, weights), rhs)
        turn = (((0,), (0,)), ((), ()))
        total = jnp.zeros((8, 512), F32)
        for lhs in (lhs_even, lhs_odd):
            centred = lax.dot_general(lhs[r], rhs[...], turn, preferred_element_type=F32)
            total = total + fold_rows(centred * centred)
        inv = lax.rsqrt(jnp.sum(total, axis=0, keepdims=True) * inv_count + 1e-05)
        inv_all[r] = inv
        factor = inv * gain
        three_parts(jnp.where(ids == 10, bias - mean * factor, weights * factor), rhs)
        for half, lhs in enumerate((lhs_even, lhs_odd)):
            shifted = lax.dot_general(lhs[r], rhs[...], turn, preferred_element_type=F32)
            for i in range(256 // CHUNK):
                value = shifted[i * CHUNK : (i + 1) * CHUNK]
                phi, grad = phi_and_slope(value)
                hidden = value * phi
                rows = pl.ds(pl.multiple_of(r * 256 + i * CHUNK, CHUNK), CHUNK)
                slope[rows, half * 512 : half * 512 + 512] = grad.astype(BF16)
                taps[rows, half * 512 : half * 512 + 512] = hidden.astype(BF16)
                if half == 0:
                    even_rows[i * CHUNK : (i + 1) * CHUNK] = hidden
        all_rows = pl.ds(pl.multiple_of(r * 256, 256), 256)
        taps[all_rows, 1024:1536] = even_rows[1:257].astype(BF16)
        return 0

    pass_on_piece(zpeer(1), across, (ypeer, partner))
    lax.fori_loop(0, 1, front, 0)
    for j in (2, 3):
        pass_on_piece(zpeer(j), grp, (corner, ypeer, xpeer, partner))
    lax.fori_loop(1, 2, front, 0)
    pass_on_piece(column(0), across, (partner,))
    pass_on_piece(column(1), grp, (partner,))
    lax.fori_loop(2, 3, front, 0)
    pass_on_piece(column(1), across, (partner,))
    lax.fori_loop(3, 4, front, 0)
    own.wait()

    def from_partner(places):
        for p in places:
            for q in (xpos * 2 + 1 - core, (1 - xpos) * 2 + 1 - core):
                arrived(conv_all.at[p, q], own_ss.at[0], conv_rs.at[p, q], partner)

    even_rows[0:8] = jnp.zeros((8, 512), F32)

    def middle(half):
        lanes = pl.ds(pl.multiple_of(half * 256, 256), 256)
        for k in range(2):
            turned[half, :, k * 128 : k * 128 + 128] = (
                conv_all[pl.ds(4 * half + 2 * k, 2)].reshape(128, 1536).T
            )
        for r in range(4):
            rows = slice(r * 256, r * 256 + 256)
            second[rows] = jnp.dot(taps[rows], turned[half], preferred_element_type=F32)

        ids = lax.broadcasted_iota(jnp.int32, (CHUNK, 256), 0).astype(F32)
        for r in range(4):
            all_rows = slice(r * 256, r * 256 + 256)
            count2 = jnp.floor((counts[r][:, 0:256] - 2.5) * 0.5) + 1.0
            for i in range(256 // CHUNK):
                valid = ids + float(i * CHUNK) < count2
                rows = slice(r * 256 + i * CHUNK, r * 256 + (i + 1) * CHUNK)
                value = second[rows]
                phi, grad = phi_and_slope(value)
                part = slice(i * CHUNK, (i + 1) * CHUNK)
                feat_rows[r, part, lanes] = jnp.where(valid, value * phi, 0.0).astype(BF16)
                back = jnp.where(valid, cot_rows[r, part, lanes].astype(F32) * grad, 0.0)
                delta[rows, lanes] = back.astype(BF16)
                even_rows[8 + i * CHUNK : 8 + (i + 1) * CHUNK, lanes] = back
            before[all_rows, lanes] = even_rows[7:263, lanes].astype(BF16)
            delta_turned[lanes, all_rows] = delta[all_rows, lanes].T

    stage = {}
    halves = (near, far)

    def weight_grad(k, b):
        half = halves[k]
        first, width = BLOCKS[b]
        cols = slice(first, first + width)
        lanes = pl.ds(pl.multiple_of(half * 256, 256), 256)
        part = jnp.dot(delta_turned[lanes, :], taps[:, cols], preferred_element_type=F32)
        part = part.reshape(4, 2, 2, 16, width)
        own_dp = pl.ds(half * 4, 4)
        gc_full[own_dp, :, :, :, cols] = part
        gc_send[own_dp, :, :, :, cols] = part.astype(BF16)
        stage[k, b] = remote(
            gc_send.at[own_dp, :, 1 - core, :, cols],
            gc_r1.at[own_dp, :, :, cols],
            s1_ss.at[k, b],
            s1_rs.at[k, b],
            partner,
        )
        stage[k, b].start()

    def reduce_core(k, b):
        half = halves[k]
        first, width = BLOCKS[b]
        cols = slice(first, first + width)
        stage[k, b].wait()
        for j in (3, 1, 2, 0):
            x_at = xpos if j % 2 == 0 else 1 - xpos
            y_at = ypos if j // 2 == 0 else 1 - ypos
            for step in range(2):
                z = half * 2 + step
                d = z * 2 + y_at
                total = gc_full[d, x_at, core, :, cols] + gc_r1[d, x_at, :, cols].astype(F32)
                if j == 0:
                    gc_k2[z, :, cols] = total
                else:
                    gc_s2[j, z, :, cols] = total.astype(BF16)
            if j > 0:
                pair = pl.ds(half * 2, 2)
                send(
                    gc_s2.at[j, pair, :, cols],
                    gc_r2.at[j, pair, :, cols],
                    s2_ss.at[k, b, j],
                    s2_rs.at[k, b, j],
                    plane[j],
                )

    def reduce_plane(k, b):
        half = halves[k]
        first, width = BLOCKS[b]
        cols = slice(first, first + width)
        pair = pl.ds(half * 2, 2)
        for j in range(1, 4):
            arrived(gc_r2.at[j, pair, :, cols], s2_ss.at[k, b, j], s2_rs.at[k, b, j], plane[j])
        for step in range(2):
            z = half * 2 + step
            total = gc_k2[z, :, cols]
            for j in range(1, 4):
                total = total + gc_r2[j, z, :, cols].astype(F32)
            gc_k3[z, :, cols] = total
            gc_s3[z, :, cols] = total.astype(BF16)
        for j in (1,) if k == 0 else (3, 2):
            zp = lines[j]
            send(
                gc_s3.at[zp, :, cols],
                gc_r3.at[zpos, :, cols],
                s3_ss.at[b, j],
                s3_rs.at[b, zpos],
                (zp * 2 + ypos, grp),
            )

    def reduce_line(b):
        first, width = BLOCKS[b]
        cols = slice(first, first + width)
        total = gc_k3[zpos, :, cols]
        for j in range(1, 4):
            zp = lines[j]
            arrived(gc_r3.at[zp, :, cols], s3_ss.at[b, j], s3_rs.at[b, zp], (zp * 2 + ypos, grp))
            total = total + gc_r3[zp, :, cols].astype(F32)
        gc_out[grp, :, cols] = total.astype(BF16)
        for j in range(1, 4):
            piece = gc_out.at[grp, :, cols]
            send(piece, piece, s4_ss.at[b, j], s4_rs.at[b, grp], (dp, (grp + j) % 4))

    def gathered(b):
        first, width = BLOCKS[b]
        cols = slice(first, first + width)
        for j in range(1, 4):
            p = (grp + j) % 4
            arrived(gc_out.at[p, :, cols], s4_ss.at[b, j], s4_rs.at[b, p], (dp, p))
        gconv_ref[:, cols] = gc_out[:, :, cols].astype(F32).reshape(64, width)

    def backward(r):
        rows = slice(r * 256, r * 256 + 256)
        weights = conv_all[...].reshape(512, 1536)
        even = jnp.dot(delta[rows, :], weights[:, 0:512], preferred_element_type=F32) + jnp.dot(
            before[rows, :], weights[:, 1024:1536], preferred_element_type=F32
        )
        odd = jnp.dot(delta[rows, :], weights[:, 512:1024], preferred_element_type=F32)
        even = (even * slope[rows, 0:512].astype(F32)).astype(BF16)
        odd = (odd * slope[rows, 512:1024].astype(F32)).astype(BF16)
        found = jnp.dot(lhs_even[r, 0:16], even, preferred_element_type=F32) + jnp.dot(
            lhs_odd[r, 0:16], odd, preferred_element_type=F32
        )
        inv_count, inv, mean = 1.0 / counts[r], inv_all[r], means[r]
        plain = found[10:11]
        with_normed = inv * (
            jnp.sum(first16[...].astype(F32) * found, axis=0, keepdims=True) - mean * plain
        )
        tap_sums = gram[r][:, 10:11]
        grads = (inv * gain_ref[...]) * (
            found - tap_sums * (plain * inv_count) - cross[r] * (with_normed * inv * inv_count)
        )
        ids = lax.broadcasted_iota(jnp.int32, (16, 512), 0)
        grads = jnp.where(ids == 10, with_normed, jnp.where(ids == 11, plain, grads))
        acc[...] += grads

    blocks = range(len(BLOCKS))
    from_partner((column(0), zpeer(1), column(1)))
    middle(near)
    for j in (2, 3):
        pass_on_piece(zpeer(j), across, (partner,))
        pass_on_piece(column(j), grp, (partner,))
        pass_on_piece(column(j), across, (partner,))
    for b in blocks:
        weight_grad(0, b)
        if b > 0:
            reduce_core(0, b - 1)
    from_partner((zpeer(2), zpeer(3), column(2), column(3)))
    reduce_core(0, len(BLOCKS) - 1)
    middle(far)
    for b in blocks:
        weight_grad(1, b)
        if b > 0:
            reduce_core(1, b - 1)
    backward(0)
    reduce_core(1, len(BLOCKS) - 1)
    backward(1)
    backward(2)
    reduce_plane(0, 0)
    backward(3)
    reduce_plane(0, 1)

    total = acc[...]
    sm_half[0] = total[:, 0:256]
    sm_half[1] = total[:, 256:512]
    small = remote(sm_half.at[1 - core], sm_core, sc_ss, sc_rs, partner)
    small.start()
    reduce_plane(0, 2)
    small.wait()
    here = xpos * 2 + ypos
    sm_xy[here] = sm_half[core] + sm_core[...]
    for j in range(1, 4):
        send(sm_xy.at[here], sm_xy.at[here], sxy_ss.at[j], sxy_rs.at[j], plane[j])

    def join_rows(i, _):
        part = pl.ds(pl.multiple_of(i * CHUNK, CHUNK), CHUNK)
        parts = [feat_rows[r, part].astype(F32) for r in range(4)]
        feat_wide[part] = jnp.stack(parts, axis=1).astype(BF16)
        return 0

    lax.fori_loop(0, 256 // CHUNK, join_rows, 0)
    feat_out = pltpu.make_async_copy(feat_wide.at[0:255], feat_ref, feat_sem)
    feat_out.start()
    for b in blocks:
        reduce_plane(1, b)
    there = ((1 - xpos) * 2 + ypos, xpos * 2 + 1 - ypos, (1 - xpos) * 2 + 1 - ypos)
    for j in range(1, 4):
        arrived(sm_xy.at[there[j - 1]], sxy_ss.at[j], sxy_rs.at[j], plane[j])
    sm_z[zpos] = (sm_xy[0] + sm_xy[1]) + (sm_xy[2] + sm_xy[3])
    for j in (3, 2, 1):
        zp = lines[j]
        send(sm_z.at[zpos], sm_z.at[zpos], sz_ss.at[j], sz_rs.at[zpos], (zp * 2 + ypos, grp))
    for b in blocks:
        reduce_line(b)
    for j in range(1, 4):
        zp = (zpos + j) % 4
        arrived(sm_z.at[zp], sz_ss.at[j], sz_rs.at[zp], (zp * 2 + ypos, grp))
    sm_out[core] = (sm_z[0] + sm_z[1]) + (sm_z[2] + sm_z[3])
    last = remote(sm_out.at[core], sm_out.at[core], so_ss, so_rs.at[core], partner)
    last.start()
    for b in range(len(BLOCKS)):
        gathered(b)
    arrived(sm_out.at[1 - core], so_ss, so_rs.at[1 - core], partner)
    small_sum = jnp.concatenate([sm_out[0], sm_out[1]], axis=1)
    ggain_ref[...] = small_sum[10:11]
    gbias_ref[...] = small_sum[11:12]
    gfirst_ref[...] = pltpu.roll(small_sum, (8 - dp) % 8 * 64, 1)[0:10, 0:64]
    feat_out.wait()
    last.wait_send()
    for c in sends:
        c.wait_send()


def pass_on(*refs):
    sources, targets, buffers, (in_sem, out_sem) = refs[0:5], refs[5:10], refs[10:15], refs[15:17]
    spans = [(0, pl.ds(0, 64)), (0, pl.ds(64, 64)), (0, pl.ds(128, 64)), (0, pl.ds(192, 63))]
    views = [tuple(group[k].at[span] for group in (sources, buffers, targets)) for k, span in spans]
    views += [(sources[k], buffers[k], targets[k]) for k in range(1, 5)]
    reads, writes = [], []
    for k, (source, buffer, target) in enumerate(views):
        c = pltpu.make_async_copy(source, buffer, in_sem.at[k])
        c.start()
        reads.append(c)
    for k, (source, buffer, target) in enumerate(views):
        reads[k].wait()
        c = pltpu.make_async_copy(buffer, target, out_sem.at[k])
        c.start()
        writes.append(c)
    for c in writes:
        c.wait()


def local_fused(
    waveform, lengths, packing, first_weight, norm_gain, norm_bias, conv_weight, grad_features
):
    vmem = lambda *shape: pltpu.VMEM(shape, F32)
    vmem16 = lambda *shape: pltpu.VMEM(shape, BF16)
    dma = pltpu.SemaphoreType.DMA
    n = len(BLOCKS)
    features, grad_conv, grad_first, grad_gain, grad_bias = pl.pallas_call(
        fused_kernel,
        out_shape=(
            jax.ShapeDtypeStruct((255, 4, 512), BF16),
            jax.ShapeDtypeStruct((64, 1536), F32),
            jax.ShapeDtypeStruct((10, 64), F32),
            jax.ShapeDtypeStruct((1, 512), F32),
            jax.ShapeDtypeStruct((1, 512), F32),
        ),
        in_specs=[pl.BlockSpec(memory_space=pl.ANY)] * 8,
        out_specs=[pl.BlockSpec(memory_space=pl.ANY)] + [pl.BlockSpec(memory_space=pltpu.VMEM)] * 4,
        scratch_shapes=[
            vmem16(4, 2560), pltpu.VMEM((1, 4), jnp.int32), pltpu.VMEM((1, 4), jnp.int32), vmem16(10, 64),
            vmem(1, 512), vmem(1, 512), vmem(2560, 128), vmem(2, 128, 128), vmem16(4, 16, 256), vmem16(16, 128),
            vmem(1024, 256), dma((6,)),
            vmem16(4, 4, 16, 256), vmem16(8, 16, 128), vmem16(16, 512), vmem16(8, 4, 16, 1536), vmem16(2, 1536, 256),
            vmem16(1024, 1024), vmem16(1024, 1536), vmem(264, 512), vmem16(1024, 512), vmem16(1024, 512),
            vmem16(512, 1024),
            vmem16(256, 4, 512), vmem16(4, 256, 512), vmem16(256, 4, 512), vmem16(4, 256, 512),
            vmem16(4, 48, 256), vmem16(4, 48, 256), vmem16(48, 512), vmem(4, 1, 512), vmem(4, 1, 512),
            vmem(4, 1, 512), vmem(4, 16, 16), vmem(4, 16, 512), vmem(16, 512),
            vmem(8, 2, 2, 16, 1536), vmem16(8, 2, 2, 16, 1536), vmem16(8, 2, 16, 1536),
            vmem(4, 16, 1536), vmem16(4, 4, 16, 1536), vmem16(4, 4, 16, 1536),
            vmem(4, 16, 1536), vmem16(4, 16, 1536), vmem16(4, 16, 1536), vmem16(4, 16, 1536),
            vmem(2, 16, 256), vmem(16, 256), vmem(4, 16, 256), vmem(4, 16, 256), vmem(2, 16, 256),
            dma((4,)), dma((4,)), dma((8,)), dma((8,)), dma((5,)), dma((24,)), dma((8, 4)),
            dma, dma, dma,
            dma((2, n)), dma((2, n)), dma((2, n, 4)), dma((2, n, 4)), dma((n, 4)), dma((n, 4)), dma((n, 4)), dma((n, 4)),
            dma, dma, dma((4,)), dma((4,)), dma((4,)), dma((4,)), dma, dma((2,)),
        ],
        compiler_params=pltpu.CompilerParams(
            collective_id=0, has_side_effects=True, vmem_limit_bytes=60 * 1024 * 1024
        ),
    )(
        waveform, lengths[None], packing[None], first_weight.T, conv_weight.reshape(4, 16, 1536),
        norm_gain[None], norm_bias[None], grad_features.transpose(1, 0, 2),
    )
    results = (features, grad_conv, grad_first, grad_gain, grad_bias)
    features, grad_conv, grad_first, grad_gain, grad_bias = pl.pallas_call(
        pass_on,
        out_shape=tuple(jax.ShapeDtypeStruct(each.shape, each.dtype) for each in results),
        in_specs=[pl.BlockSpec(memory_space=pl.ANY)] * 5,
        out_specs=[pl.BlockSpec(memory_space=pl.ANY)] * 5,
        scratch_shapes=[pltpu.VMEM(each.shape, each.dtype) for each in results] + [dma((8,)), dma((8,))],
    )(*results)
    return (features.transpose(1, 0, 2), grad_conv, grad_first.T, grad_gain[0], grad_bias[0])


def solution(mesh):
    shape = dict(mesh.shape)
    fused = shape["dp"] == 8 and shape["group"] == 4
    return jax.shard_map(
        local_fused if fused else local,
        mesh=mesh,
        in_specs=(
            P(("dp", "group"), None),
            P(("dp", "group")),
            P(("dp", "group")),
            P("dp", None),
            P(),
            P(),
            P("dp", None),
            P(("dp", "group"), None, None),
        ),
        out_specs=(P(("dp", "group"), None, None), P("dp", None), P("dp", None), P(), P()),
        check_vma=False,
    )
```

```python
import functools

import jax
import jax.numpy as jnp
from jax import lax
from jax.experimental import pallas as pl
from jax.experimental.pallas import tpu as pltpu
from jax.sharding import PartitionSpec as P

MESH = pl.DeviceIdType.MESH
F32, BF16 = jnp.float32, jnp.bfloat16
CHUNK = 32


def gelu_slope(values):
    return (
        0.5 * (1.0 + lax.erf(values * 0.7071067811865476))
        + values * jnp.exp(-0.5 * values * values) * 0.3989422804014327
    )


def tap_matrix(hidden, frames_second):
    row_count, frames_first, channels = hidden.shape
    zero_frame = jnp.zeros((row_count, 1, channels), hidden.dtype)
    paired = jnp.concatenate([hidden, zero_frame], axis=1).reshape(
        row_count, frames_second + 1, 2, channels
    )
    even_half = paired[:, :, 0]
    odd_half = paired[:, :, 1]
    stacked = jnp.concatenate(
        [even_half[:, :frames_second], odd_half[:, :frames_second], even_half[:, 1:]], axis=2
    )
    return stacked.reshape(row_count * frames_second, 3 * channels)


def spread_back(back_taps, row_count, frames_second, frames_first):
    first_tap = back_taps[0].reshape(row_count, frames_second, -1)
    middle_tap = back_taps[1].reshape(row_count, frames_second, -1)
    last_tap = back_taps[2].reshape(row_count, frames_second, -1)
    channels = first_tap.shape[2]
    zero_frame = jnp.zeros((row_count, 1, channels), jnp.float32)
    even_half = jnp.concatenate([first_tap, zero_frame], axis=1) + jnp.concatenate(
        [zero_frame, last_tap], axis=1
    )
    odd_half = jnp.concatenate([middle_tap, zero_frame], axis=1)
    joined = jnp.stack([even_half, odd_half], axis=2).reshape(
        row_count, 2 * frames_second + 2, channels
    )
    return joined[:, :frames_first]


def local(
    waveform, lengths, packing, first_weight, norm_gain, norm_bias, conv_weight, grad_features
):
    row_count, capacity = waveform.shape
    channels = norm_gain.shape[0]
    frames_first = capacity // 5 - 1
    frames_second = (capacity // 5 - 2) // 2
    groups = lax.axis_size("group")
    own_group = lax.axis_index("group")
    group_rows = groups * row_count
    all_pack, all_lengths = (
        lax.all_gather(packing, "group", axis=0, tiled=True),
        lax.all_gather(lengths, "group", axis=0, tiled=True),
    )
    target = all_pack // row_count
    slot_index = all_pack % row_count
    positions = jnp.arange(group_rows)
    source = positions // row_count
    same_source = source[:, None] == source[None, :]
    same_target = target[:, None] == target[None, :]
    before = positions[:, None] > positions[None, :]
    rank_among = jnp.sum((same_source & same_target & before).astype(jnp.int32), axis=1)
    arriving = target == own_group
    slot_ids = jnp.arange(row_count)
    choose_slot = (slot_index[None, :] == slot_ids[:, None]) & arriving[None, :]
    local_lengths = jnp.sum(jnp.where(choose_slot, all_lengths[None, :], 0), axis=1)
    per_peer = 2 * ((row_count + 2 * groups - 1) // (2 * groups))
    lane_ids = jnp.arange(per_peer)
    own_target = lax.dynamic_slice_in_dim(target, own_group * row_count, row_count)
    own_rank = lax.dynamic_slice_in_dim(rank_among, own_group * row_count, row_count)
    outgoing = (
        (own_target[None, None, :] == jnp.arange(groups)[:, None, None])
        & (own_rank[None, None, :] == lane_ids[None, :, None])
    ).astype(jnp.bfloat16)
    send_rows = jnp.einsum(
        "gkr,rs->gks", outgoing, waveform, preferred_element_type=jnp.float32
    ).astype(jnp.bfloat16)
    received = lax.all_to_all(send_rows, "group", split_axis=0, concat_axis=0, tiled=True)
    pick_slots = (
        choose_slot[:, :, None] & (rank_among[None, :, None] == lane_ids[None, None, :])
    ).astype(jnp.float32)
    pick_slots = jnp.sum(pick_slots.reshape(row_count, groups, row_count, per_peer), axis=2).astype(
        jnp.bfloat16
    )
    wave_rows = jnp.einsum(
        "lsk,skn->ln", pick_slots, received, preferred_element_type=jnp.float32
    ).astype(jnp.bfloat16)
    first_whole = lax.all_gather(first_weight, "dp", axis=0, tiled=True)
    in_length = jnp.arange(capacity)[None, :] < local_lengths[:, None]
    masked = jnp.where(in_length, wave_rows, jnp.zeros_like(wave_rows))
    blocks = masked.reshape(row_count, capacity // 5, 5)
    taps_first = jnp.concatenate([blocks[:, :-1], blocks[:, 1:]], axis=2).reshape(
        row_count * frames_first, 10
    )
    conv_first = lax.dot_general(
        taps_first, first_whole, (((1,), (1,)), ((), ())), preferred_element_type=jnp.float32
    )
    conv_first = conv_first.reshape(row_count, frames_first, channels)
    count_first = (local_lengths - 10) // 5 + 1
    count_second = (count_first - 3) // 2 + 1
    valid_first = (jnp.arange(frames_first)[None, :] < count_first[:, None]).astype(jnp.float32)[
        :, :, None
    ]
    valid_second = (jnp.arange(frames_second)[None, :] < count_second[:, None]).astype(jnp.float32)[
        :, :, None
    ]
    count_float = count_first.astype(jnp.float32)[:, None, None]
    row_mean = jnp.sum(conv_first * valid_first, axis=1, keepdims=True) / count_float
    centred = (conv_first - row_mean) * valid_first
    row_var = jnp.sum(centred * centred, axis=1, keepdims=True) / count_float
    inv_scale = lax.rsqrt(row_var + 1e-05)
    normed = (conv_first - row_mean) * inv_scale
    shifted = normed * norm_gain + norm_bias
    hidden = (jax.nn.gelu(shifted, approximate=False) * valid_first).astype(jnp.bfloat16)
    taps_second = tap_matrix(hidden, frames_second)
    conv_whole = lax.all_gather(conv_weight, "dp", axis=0, tiled=True)
    conv_second = lax.dot_general(
        taps_second, conv_whole, (((1,), (1,)), ((), ())), preferred_element_type=jnp.float32
    )
    conv_second = conv_second.reshape(row_count, frames_second, channels)
    features = (jax.nn.gelu(conv_second, approximate=False) * valid_second).astype(jnp.bfloat16)
    delta_second = (
        grad_features.astype(jnp.float32) * valid_second * gelu_slope(conv_second)
    ).astype(jnp.bfloat16)
    delta_flat = delta_second.reshape(row_count * frames_second, channels)
    back_taps = tuple(
        (
            jnp.dot(
                delta_flat,
                conv_whole[:, tap_index * channels : (tap_index + 1) * channels],
                preferred_element_type=jnp.float32,
            )
            for tap_index in range(3)
        )
    )
    share = lax.psum_scatter(
        lax.dot_general(
            delta_flat, taps_second, (((0,), (0,)), ((), ())), preferred_element_type=jnp.float32
        ),
        "dp",
        scatter_dimension=0,
        tiled=True,
    )
    grad_conv = lax.psum(share, "group")
    delta_hidden = spread_back(back_taps, row_count, frames_second, frames_first)
    delta_norm = delta_hidden * valid_first * gelu_slope(shifted)
    gain_term = jnp.sum(delta_norm * normed, axis=(0, 1))
    bias_term = jnp.sum(delta_norm, axis=(0, 1))
    scaled = delta_norm * norm_gain
    mean_grad = jnp.sum(scaled, axis=1, keepdims=True) / count_float
    mean_cross = jnp.sum(scaled * normed, axis=1, keepdims=True) / count_float
    delta_first = ((scaled - mean_grad - normed * mean_cross) * inv_scale * valid_first).astype(
        jnp.bfloat16
    )
    first_term = lax.dot_general(
        delta_first.reshape(row_count * frames_first, channels),
        taps_first,
        (((0,), (0,)), ((), ())),
        preferred_element_type=jnp.float32,
    )
    stacked = jnp.concatenate([first_term, gain_term[:, None], bias_term[:, None]], axis=1)
    summed = lax.psum(stacked, ("dp", "group"))
    shard_rows = channels // lax.axis_size("dp")
    grad_first = lax.dynamic_slice_in_dim(
        summed[:, :10], lax.axis_index("dp") * shard_rows, shard_rows, 0
    )
    return (features, grad_conv, grad_first, summed[:, 10], summed[:, 11])


BLOCKS = ((0, 512), (512, 512), (1024, 512))


def phi_and_slope(values):
    phi = 0.5 + 0.5 * lax.erf(values * 0.7071067811865476)
    return phi, phi + (values * 0.3989422804014327) * jnp.exp2(values * values * -0.7213475204444817)


def fold_rows(block):
    return jnp.sum(block.reshape(block.shape[0] // 8, 8, block.shape[1]), axis=0)


def three_parts(values, out):
    high = values.astype(BF16)
    rest = values - high.astype(F32)
    middle = rest.astype(BF16)
    out[0:16] = high
    out[16:32] = middle
    out[32:48] = (rest - middle.astype(F32)).astype(BF16)


def fused_kernel(
    wave_in, lengths_in, packing_in, first_in, conv_ref, gain_in, bias_in, cot_ref,
    feat_ref, gconv_ref, gfirst_ref, ggain_ref, gbias_ref,
    wave_own, lengths_own, packing_own, first_own, gain_ref, bias_ref, wide, narrow, wave_ref, first_ref, second, in_sem,
    rows_all, first_all, first16, conv_all, turned, slope, taps, even_rows, delta, before, delta_turned,
    cot_wide, cot_rows, feat_wide, feat_rows, lhs_even, lhs_odd, rhs, counts, means, inv_all, gram, cross, acc,
    gc_full, gc_send, gc_r1, gc_k2, gc_s2, gc_r2, gc_k3, gc_s3, gc_r3, gc_out,
    sm_half, sm_core, sm_xy, sm_z, sm_out,
    row_ss, row_rs, first_ss, first_rs, own_ss, fw_ss, conv_rs, own_sem, cot_sem, feat_sem,
    s1_ss, s1_rs, s2_ss, s2_rs, s3_ss, s3_rs, s4_ss, s4_rs,
    sc_ss, sc_rs, sxy_ss, sxy_rs, sz_ss, sz_rs, so_ss, so_rs,
):
    dp, grp = lax.axis_index("dp"), lax.axis_index("group")
    core, xpos = grp % 2, grp // 2
    ypos, zpos = dp % 2, dp // 2
    partner = (dp, xpos * 2 + (1 - core))
    xpeer = (dp, (1 - xpos) * 2 + core)
    ypeer = (zpos * 2 + (1 - ypos), grp)
    corner = (zpos * 2 + (1 - ypos), (1 - xpos) * 2 + core)
    plane = (None, xpeer, ypeer, corner)

    lines = (zpos, zpos + 1 - 2 * (zpos % 2), (zpos + 2) % 4, 3 - zpos)
    near = zpos // 2
    far = 1 - near

    def zpeer(j):
        return lines[j] * 2 + ypos

    def remote(src, dst, ss, rs, dev):
        return pltpu.make_async_remote_copy(
            src_ref=src, dst_ref=dst, send_sem=ss, recv_sem=rs, device_id=dev, device_id_type=MESH
        )

    sends = []

    def send(src, dst, ss, rs, dev):
        c = remote(src, dst, ss, rs, dev)
        c.start()
        sends.append(c)

    def arrived(ref, ss, rs, dev):
        remote(ref, ref, ss, rs, dev).wait_recv()

    cot_in = pltpu.make_async_copy(cot_ref, cot_wide.at[0:255], cot_sem)
    barrier = pltpu.get_barrier_semaphore()
    for j in (3, 2, 1):
        for y_at in (1 - ypos, ypos):
            pl.semaphore_signal(barrier, inc=1, device_id=(lines[j] * 2 + y_at, grp), device_id_type=MESH)
    for device in (corner, ypeer, xpeer, partner, (dp, (1 - xpos) * 2 + 1 - core)):
        pl.semaphore_signal(barrier, inc=1, device_id=device, device_id_type=MESH)
    own = pltpu.make_async_copy(conv_ref, conv_all.at[dp], own_sem)
    own.start()
    loads = []
    pairs = (
        (wave_in, wave_own), (first_in, first_own), (lengths_in, lengths_own), (packing_in, packing_own),
        (gain_in, gain_ref), (bias_in, bias_ref),
    )
    for k, (source, target) in enumerate(pairs):
        c = pltpu.make_async_copy(source, target, in_sem.at[k])
        c.start()
        loads.append(c)
    cot_in.start()
    cot_wide[255] = jnp.zeros((4, 512), BF16)
    even_rows[256:264] = jnp.zeros((8, 512), F32)
    acc[...] = jnp.zeros_like(acc)
    for c in loads:
        c.wait()
    piece = first_own[...].astype(F32)
    piece = jnp.concatenate([piece, jnp.zeros((6, 64), F32)], axis=0)
    piece = jnp.concatenate([piece, piece], axis=1)
    lane = lax.broadcasted_iota(jnp.int32, (16, 128), 1)
    piece = jnp.where(lane // 64 == dp % 2, piece, 0.0).astype(BF16)
    first_ref[...] = piece
    first_all[dp] = piece
    wave = wave_own[...].astype(F32)
    wave = jnp.concatenate([wave, wave], axis=0)
    wide[...] = jnp.concatenate([wave] * 16, axis=0).T
    lane = lax.broadcasted_iota(jnp.int32, (256, 128), 1) // 4
    taken = jnp.zeros((256, 128), F32)
    for k in range(10):
        taken = jnp.where(lane == k, wide[pl.ds(k, 256, stride=10), :], taken)
    narrow[0] = taken[0:128].T
    narrow[1] = taken[128:256].T
    row_ids = lax.broadcasted_iota(jnp.int32, (16, 256), 0)
    for r in range(4):
        place = packing_own[0:1, r : r + 1]
        length = lengths_own[0:1, r : r + 1]
        notes = jnp.where(row_ids == 10, place, jnp.where(row_ids == 11, length // 16, length % 16)).astype(F32)
        block = jnp.concatenate([narrow[0, pl.ds(r, 16, stride=4), :], narrow[1, pl.ds(r, 16, stride=4), :]], axis=1)
        block = jnp.where(row_ids < 10, block, notes).astype(BF16)
        wave_ref[r] = block
        rows_all[grp, r] = block
    pl.semaphore_wait(barrier, 11)

    for j in (3, 2, 1, 0):
        for y_at in (1 - ypos, ypos) if j > 0 else (1 - ypos,):
            peer = (lines[j] * 2 + y_at, grp)
            send(first_ref, first_all.at[dp], first_ss.at[2 * j + (0 if y_at is ypos else 1)], first_rs.at[dp], peer)
    for j in range(1, 4):
        send(wave_ref, rows_all.at[grp], row_ss.at[j], row_rs.at[grp], (dp, (grp + j) % 4))
    mine = conv_ref.at[grp]
    across = (1 - xpos) * 2 + core
    send(mine, conv_all.at[dp, grp], own_ss.at[0], conv_rs.at[dp, grp], ypeer)
    send(mine, conv_all.at[dp, grp], own_ss.at[1], conv_rs.at[dp, grp], (zpeer(1), grp))
    send(conv_ref.at[across], conv_all.at[dp, across], own_ss.at[4], conv_rs.at[dp, across], (zpeer(1), grp))
    for j in (2, 3):
        send(mine, conv_all.at[dp, grp], own_ss.at[j], conv_rs.at[dp, grp], (zpeer(j), grp))
    passed = []

    def pass_on_piece(p, q, devices):
        piece = conv_all.at[p, q]
        arrived(piece, own_ss.at[0], conv_rs.at[p, q], xpeer)
        for device in devices:
            send(piece, piece, fw_ss.at[len(passed)], conv_rs.at[p, q], device)
            passed.append(device)

    def column(j):
        return lines[j] * 2 + 1 - ypos

    cot_in.wait()

    def split_rows(i, _):
        part = pl.ds(pl.multiple_of(i * CHUNK, CHUNK), CHUNK)
        block = cot_wide[part].astype(F32)
        for r in range(4):
            cot_rows[r, part] = block[:, r, :].astype(BF16)
        return 0

    lax.fori_loop(0, 256 // CHUNK, split_rows, 0)

    pass_on_piece(column(0), grp, (xpeer, partner))
    pass_on_piece(zpeer(1), grp, (ypeer, partner))

    for j in range(1, 4):
        p = (grp + j) % 4
        arrived(rows_all.at[p], row_ss.at[j], row_rs.at[p], (dp, p))

    pair_ids = lax.broadcasted_iota(jnp.int32, (16, 256), 1).astype(F32) * 2.0
    for r in range(4):
        place = (grp * 4 + r).astype(F32)
        chosen = jnp.zeros((16, 256), F32)
        for s in range(4):
            for i in range(4):
                row = rows_all[s, i].astype(F32)
                chosen = chosen + row * (row[10:11] == place).astype(F32)
        length = chosen[11:12] * 16.0 + chosen[12:13]
        count = jnp.floor((length - 9.5) * 0.2) + 1.0
        counts[r] = jnp.concatenate([count, count], axis=1)
        one = jnp.where(row_ids == 10, 1.0, 0.0)
        even = jnp.where(row_ids < 10, chosen, one)
        following = pltpu.roll(pltpu.roll(chosen, 255, 1), 5, 0)
        odd = jnp.where(row_ids < 5, pltpu.roll(chosen, 11, 0), jnp.where(row_ids < 10, following, one))
        even = jnp.where(pair_ids < count, even, 0.0).astype(BF16)
        odd = jnp.where(pair_ids + 1.0 < count, odd, 0.0).astype(BF16)
        for k in range(3):
            lhs_even[r, 16 * k : 16 * k + 16] = even
            lhs_odd[r, 16 * k : 16 * k + 16] = odd
        inner = (((1,), (1,)), ((), ()))
        gram[r] = lax.dot_general(even, even, inner, preferred_element_type=F32) + lax.dot_general(
            odd, odd, inner, preferred_element_type=F32
        )

    for j in range(1, 8):
        p = (dp + j) % 8
        arrived(first_all.at[p], first_ss.at[j], first_rs.at[p], (p, grp))
    for b in range(4):
        first16[:, b * 128 : b * 128 + 128] = first_all[2 * b] + first_all[2 * b + 1]

    def front(r, _):
        weights = first16[...].astype(F32)
        gain, bias = gain_ref[...], bias_ref[...]
        inv_count = 1.0 / counts[r]
        tap_sums = gram[r][:, 10:11]
        mean = jnp.sum(weights * tap_sums, axis=0, keepdims=True) * inv_count
        means[r] = mean
        centre = gram[r] - tap_sums * gram[r][10:11, :] * inv_count[:, 0:16]
        high = centre.astype(BF16)
        rest = centre - high.astype(F32)
        middle_part = rest.astype(BF16)
        low = (rest - middle_part.astype(F32)).astype(BF16)
        taps16 = first16[...]
        cross[r] = (
            jnp.dot(high, taps16, preferred_element_type=F32)
            + jnp.dot(middle_part, taps16, preferred_element_type=F32)
        ) + jnp.dot(low, taps16, preferred_element_type=F32)
        ids = lax.broadcasted_iota(jnp.int32, (16, 512), 0)
        three_parts(jnp.where(ids == 10, -mean, weights), rhs)
        turn = (((0,), (0,)), ((), ()))
        total = jnp.zeros((8, 512), F32)
        for lhs in (lhs_even, lhs_odd):
            centred = lax.dot_general(lhs[r], rhs[...], turn, preferred_element_type=F32)
            total = total + fold_rows(centred * centred)
        inv = lax.rsqrt(jnp.sum(total, axis=0, keepdims=True) * inv_count + 1e-05)
        inv_all[r] = inv
        factor = inv * gain
        three_parts(jnp.where(ids == 10, bias - mean * factor, weights * factor), rhs)
        for half, lhs in enumerate((lhs_even, lhs_odd)):
            shifted = lax.dot_general(lhs[r], rhs[...], turn, preferred_element_type=F32)
            for i in range(256 // CHUNK):
                value = shifted[i * CHUNK : (i + 1) * CHUNK]
                phi, grad = phi_and_slope(value)
                hidden = value * phi
                rows = pl.ds(pl.multiple_of(r * 256 + i * CHUNK, CHUNK), CHUNK)
                slope[rows, half * 512 : half * 512 + 512] = grad.astype(BF16)
                taps[rows, half * 512 : half * 512 + 512] = hidden.astype(BF16)
                if half == 0:
                    even_rows[i * CHUNK : (i + 1) * CHUNK] = hidden
        all_rows = pl.ds(pl.multiple_of(r * 256, 256), 256)
        taps[all_rows, 1024:1536] = even_rows[1:257].astype(BF16)
        return 0

    pass_on_piece(zpeer(1), across, (ypeer, partner))
    lax.fori_loop(0, 1, front, 0)
    for j in (2, 3):
        pass_on_piece(zpeer(j), grp, (corner, ypeer, xpeer, partner))
    lax.fori_loop(1, 2, front, 0)
    pass_on_piece(column(0), across, (partner,))
    pass_on_piece(column(1), grp, (partner,))
    lax.fori_loop(2, 3, front, 0)
    pass_on_piece(column(1), across, (partner,))
    lax.fori_loop(3, 4, front, 0)
    own.wait()

    def from_partner(places):
        for p in places:
            for q in (xpos * 2 + 1 - core, (1 - xpos) * 2 + 1 - core):
                arrived(conv_all.at[p, q], own_ss.at[0], conv_rs.at[p, q], partner)

    even_rows[0:8] = jnp.zeros((8, 512), F32)

    def middle(half):
        lanes = pl.ds(pl.multiple_of(half * 256, 256), 256)
        for k in range(2):
            turned[half, :, k * 128 : k * 128 + 128] = (
                conv_all[pl.ds(4 * half + 2 * k, 2)].reshape(128, 1536).T
            )
        for r in range(4):
            rows = slice(r * 256, r * 256 + 256)
            second[rows] = jnp.dot(taps[rows], turned[half], preferred_element_type=F32)

        ids = lax.broadcasted_iota(jnp.int32, (CHUNK, 256), 0).astype(F32)
        for r in range(4):
            all_rows = slice(r * 256, r * 256 + 256)
            count2 = jnp.floor((counts[r][:, 0:256] - 2.5) * 0.5) + 1.0
            for i in range(256 // CHUNK):
                valid = ids + float(i * CHUNK) < count2
                rows = slice(r * 256 + i * CHUNK, r * 256 + (i + 1) * CHUNK)
                value = second[rows]
                phi, grad = phi_and_slope(value)
                part = slice(i * CHUNK, (i + 1) * CHUNK)
                feat_rows[r, part, lanes] = jnp.where(valid, value * phi, 0.0).astype(BF16)
                back = jnp.where(valid, cot_rows[r, part, lanes].astype(F32) * grad, 0.0)
                delta[rows, lanes] = back.astype(BF16)
                even_rows[8 + i * CHUNK : 8 + (i + 1) * CHUNK, lanes] = back
            before[all_rows, lanes] = even_rows[7:263, lanes].astype(BF16)
            delta_turned[lanes, all_rows] = delta[all_rows, lanes].T

    stage = {}
    halves = (near, far)

    def weight_grad(k, b):
        half = halves[k]
        first, width = BLOCKS[b]
        cols = slice(first, first + width)
        lanes = pl.ds(pl.multiple_of(half * 256, 256), 256)
        part = jnp.dot(delta_turned[lanes, :], taps[:, cols], preferred_element_type=F32)
        part = part.reshape(4, 2, 2, 16, width)
        own_dp = pl.ds(half * 4, 4)
        gc_full[own_dp, :, :, :, cols] = part
        gc_send[own_dp, :, :, :, cols] = part.astype(BF16)
        stage[k, b] = remote(
            gc_send.at[own_dp, :, 1 - core, :, cols],
            gc_r1.at[own_dp, :, :, cols],
            s1_ss.at[k, b],
            s1_rs.at[k, b],
            partner,
        )
        stage[k, b].start()

    def reduce_core(k, b):
        half = halves[k]
        first, width = BLOCKS[b]
        cols = slice(first, first + width)
        stage[k, b].wait()
        for j in (3, 1, 2, 0):
            x_at = xpos if j % 2 == 0 else 1 - xpos
            y_at = ypos if j // 2 == 0 else 1 - ypos
            for step in range(2):
                z = half * 2 + step
                d = z * 2 + y_at
                total = gc_full[d, x_at, core, :, cols] + gc_r1[d, x_at, :, cols].astype(F32)
                if j == 0:
                    gc_k2[z, :, cols] = total
                else:
                    gc_s2[j, z, :, cols] = total.astype(BF16)
            if j > 0:
                pair = pl.ds(half * 2, 2)
                send(
                    gc_s2.at[j, pair, :, cols],
                    gc_r2.at[j, pair, :, cols],
                    s2_ss.at[k, b, j],
                    s2_rs.at[k, b, j],
                    plane[j],
                )

    def reduce_plane(k, b):
        half = halves[k]
        first, width = BLOCKS[b]
        cols = slice(first, first + width)
        pair = pl.ds(half * 2, 2)
        for j in range(1, 4):
            arrived(gc_r2.at[j, pair, :, cols], s2_ss.at[k, b, j], s2_rs.at[k, b, j], plane[j])
        for step in range(2):
            z = half * 2 + step
            total = gc_k2[z, :, cols]
            for j in range(1, 4):
                total = total + gc_r2[j, z, :, cols].astype(F32)
            gc_k3[z, :, cols] = total
            gc_s3[z, :, cols] = total.astype(BF16)
        for j in (1,) if k == 0 else (3, 2):
            zp = lines[j]
            send(
                gc_s3.at[zp, :, cols],
                gc_r3.at[zpos, :, cols],
                s3_ss.at[b, j],
                s3_rs.at[b, zpos],
                (zp * 2 + ypos, grp),
            )

    def reduce_line(b):
        first, width = BLOCKS[b]
        cols = slice(first, first + width)
        total = gc_k3[zpos, :, cols]
        for j in range(1, 4):
            zp = lines[j]
            arrived(gc_r3.at[zp, :, cols], s3_ss.at[b, j], s3_rs.at[b, zp], (zp * 2 + ypos, grp))
            total = total + gc_r3[zp, :, cols].astype(F32)
        gc_out[grp, :, cols] = total.astype(BF16)
        for j in range(1, 4):
            piece = gc_out.at[grp, :, cols]
            send(piece, piece, s4_ss.at[b, j], s4_rs.at[b, grp], (dp, (grp + j) % 4))

    def gathered(b):
        first, width = BLOCKS[b]
        cols = slice(first, first + width)
        for j in range(1, 4):
            p = (grp + j) % 4
            arrived(gc_out.at[p, :, cols], s4_ss.at[b, j], s4_rs.at[b, p], (dp, p))
        gconv_ref[:, cols] = gc_out[:, :, cols].astype(F32).reshape(64, width)

    def backward(r):
        rows = slice(r * 256, r * 256 + 256)
        weights = conv_all[...].reshape(512, 1536)
        even = jnp.dot(delta[rows, :], weights[:, 0:512], preferred_element_type=F32) + jnp.dot(
            before[rows, :], weights[:, 1024:1536], preferred_element_type=F32
        )
        odd = jnp.dot(delta[rows, :], weights[:, 512:1024], preferred_element_type=F32)
        even = (even * slope[rows, 0:512].astype(F32)).astype(BF16)
        odd = (odd * slope[rows, 512:1024].astype(F32)).astype(BF16)
        found = jnp.dot(lhs_even[r, 0:16], even, preferred_element_type=F32) + jnp.dot(
            lhs_odd[r, 0:16], odd, preferred_element_type=F32
        )
        inv_count, inv, mean = 1.0 / counts[r], inv_all[r], means[r]
        plain = found[10:11]
        with_normed = inv * (
            jnp.sum(first16[...].astype(F32) * found, axis=0, keepdims=True) - mean * plain
        )
        tap_sums = gram[r][:, 10:11]
        grads = (inv * gain_ref[...]) * (
            found - tap_sums * (plain * inv_count) - cross[r] * (with_normed * inv * inv_count)
        )
        ids = lax.broadcasted_iota(jnp.int32, (16, 512), 0)
        grads = jnp.where(ids == 10, with_normed, jnp.where(ids == 11, plain, grads))
        acc[...] += grads

    blocks = range(len(BLOCKS))
    from_partner((column(0), zpeer(1), column(1)))
    middle(near)
    for j in (2, 3):
        pass_on_piece(zpeer(j), across, (partner,))
        pass_on_piece(column(j), grp, (partner,))
        pass_on_piece(column(j), across, (partner,))
    for b in blocks:
        weight_grad(0, b)
        if b > 0:
            reduce_core(0, b - 1)
    from_partner((zpeer(2), zpeer(3), column(2), column(3)))
    reduce_core(0, len(BLOCKS) - 1)
    middle(far)
    for b in blocks:
        weight_grad(1, b)
        if b > 0:
            reduce_core(1, b - 1)
    backward(0)
    reduce_core(1, len(BLOCKS) - 1)
    backward(1)
    backward(2)
    reduce_plane(0, 0)
    backward(3)
    reduce_plane(0, 1)

    total = acc[...]
    sm_half[0] = total[:, 0:256]
    sm_half[1] = total[:, 256:512]
    small = remote(sm_half.at[1 - core], sm_core, sc_ss, sc_rs, partner)
    small.start()
    reduce_plane(0, 2)
    small.wait()
    here = xpos * 2 + ypos
    sm_xy[here] = sm_half[core] + sm_core[...]
    for j in range(1, 4):
        send(sm_xy.at[here], sm_xy.at[here], sxy_ss.at[j], sxy_rs.at[j], plane[j])

    def join_rows(i, _):
        part = pl.ds(pl.multiple_of(i * CHUNK, CHUNK), CHUNK)
        parts = [feat_rows[r, part].astype(F32) for r in range(4)]
        feat_wide[part] = jnp.stack(parts, axis=1).astype(BF16)
        return 0

    for b in blocks:
        reduce_plane(1, b)
    lax.fori_loop(0, 256 // CHUNK, join_rows, 0)
    feat_out = pltpu.make_async_copy(feat_wide.at[0:255], feat_ref, feat_sem)
    feat_out.start()
    there = ((1 - xpos) * 2 + ypos, xpos * 2 + 1 - ypos, (1 - xpos) * 2 + 1 - ypos)
    for j in range(1, 4):
        arrived(sm_xy.at[there[j - 1]], sxy_ss.at[j], sxy_rs.at[j], plane[j])
    sm_z[zpos] = (sm_xy[0] + sm_xy[1]) + (sm_xy[2] + sm_xy[3])
    for j in (3, 2, 1):
        zp = lines[j]
        send(sm_z.at[zpos], sm_z.at[zpos], sz_ss.at[j], sz_rs.at[zpos], (zp * 2 + ypos, grp))
    for b in blocks:
        reduce_line(b)
    for j in range(1, 4):
        zp = (zpos + j) % 4
        arrived(sm_z.at[zp], sz_ss.at[j], sz_rs.at[zp], (zp * 2 + ypos, grp))
    sm_out[core] = (sm_z[0] + sm_z[1]) + (sm_z[2] + sm_z[3])
    last = remote(sm_out.at[core], sm_out.at[core], so_ss, so_rs.at[core], partner)
    last.start()
    for b in range(len(BLOCKS)):
        gathered(b)
    arrived(sm_out.at[1 - core], so_ss, so_rs.at[1 - core], partner)
    small_sum = jnp.concatenate([sm_out[0], sm_out[1]], axis=1)
    ggain_ref[...] = small_sum[10:11]
    gbias_ref[...] = small_sum[11:12]
    gfirst_ref[...] = pltpu.roll(small_sum, (8 - dp) % 8 * 64, 1)[0:10, 0:64]
    feat_out.wait()
    last.wait_send()
    for c in sends:
        c.wait_send()


def pass_on(*refs):
    sources, targets, buffers, (in_sem, out_sem) = refs[0:5], refs[5:10], refs[10:15], refs[15:17]
    spans = [(0, pl.ds(0, 64)), (0, pl.ds(64, 64)), (0, pl.ds(128, 64)), (0, pl.ds(192, 63))]
    views = [tuple(group[k].at[span] for group in (sources, buffers, targets)) for k, span in spans]
    views += [(sources[k], buffers[k], targets[k]) for k in range(1, 5)]
    reads, writes = [], []
    for k, (source, buffer, target) in enumerate(views):
        c = pltpu.make_async_copy(source, buffer, in_sem.at[k])
        c.start()
        reads.append(c)
    for k, (source, buffer, target) in enumerate(views):
        reads[k].wait()
        c = pltpu.make_async_copy(buffer, target, out_sem.at[k])
        c.start()
        writes.append(c)
    for c in writes:
        c.wait()


def local_fused(
    waveform, lengths, packing, first_weight, norm_gain, norm_bias, conv_weight, grad_features
):
    vmem = lambda *shape: pltpu.VMEM(shape, F32)
    vmem16 = lambda *shape: pltpu.VMEM(shape, BF16)
    dma = pltpu.SemaphoreType.DMA
    n = len(BLOCKS)
    features, grad_conv, grad_first, grad_gain, grad_bias = pl.pallas_call(
        fused_kernel,
        out_shape=(
            jax.ShapeDtypeStruct((255, 4, 512), BF16),
            jax.ShapeDtypeStruct((64, 1536), F32),
            jax.ShapeDtypeStruct((10, 64), F32),
            jax.ShapeDtypeStruct((1, 512), F32),
            jax.ShapeDtypeStruct((1, 512), F32),
        ),
        in_specs=[pl.BlockSpec(memory_space=pl.ANY)] * 8,
        out_specs=[pl.BlockSpec(memory_space=pl.ANY)] + [pl.BlockSpec(memory_space=pltpu.VMEM)] * 4,
        scratch_shapes=[
            vmem16(4, 2560), pltpu.VMEM((1, 4), jnp.int32), pltpu.VMEM((1, 4), jnp.int32), vmem16(10, 64),
            vmem(1, 512), vmem(1, 512), vmem(2560, 128), vmem(2, 128, 128), vmem16(4, 16, 256), vmem16(16, 128),
            vmem(1024, 256), dma((6,)),
            vmem16(4, 4, 16, 256), vmem16(8, 16, 128), vmem16(16, 512), vmem16(8, 4, 16, 1536), vmem16(2, 1536, 256),
            vmem16(1024, 1024), vmem16(1024, 1536), vmem(264, 512), vmem16(1024, 512), vmem16(1024, 512),
            vmem16(512, 1024),
            vmem16(256, 4, 512), vmem16(4, 256, 512), vmem16(256, 4, 512), vmem16(4, 256, 512),
            vmem16(4, 48, 256), vmem16(4, 48, 256), vmem16(48, 512), vmem(4, 1, 512), vmem(4, 1, 512),
            vmem(4, 1, 512), vmem(4, 16, 16), vmem(4, 16, 512), vmem(16, 512),
            vmem(8, 2, 2, 16, 1536), vmem16(8, 2, 2, 16, 1536), vmem16(8, 2, 16, 1536),
            vmem(4, 16, 1536), vmem16(4, 4, 16, 1536), vmem16(4, 4, 16, 1536),
            vmem(4, 16, 1536), vmem16(4, 16, 1536), vmem16(4, 16, 1536), vmem16(4, 16, 1536),
            vmem(2, 16, 256), vmem(16, 256), vmem(4, 16, 256), vmem(4, 16, 256), vmem(2, 16, 256),
            dma((4,)), dma((4,)), dma((8,)), dma((8,)), dma((5,)), dma((24,)), dma((8, 4)),
            dma, dma, dma,
            dma((2, n)), dma((2, n)), dma((2, n, 4)), dma((2, n, 4)), dma((n, 4)), dma((n, 4)), dma((n, 4)), dma((n, 4)),
            dma, dma, dma((4,)), dma((4,)), dma((4,)), dma((4,)), dma, dma((2,)),
        ],
        compiler_params=pltpu.CompilerParams(
            collective_id=0, has_side_effects=True, vmem_limit_bytes=60 * 1024 * 1024
        ),
    )(
        waveform, lengths[None], packing[None], first_weight.T, conv_weight.reshape(4, 16, 1536),
        norm_gain[None], norm_bias[None], grad_features.transpose(1, 0, 2),
    )
    results = (features, grad_conv, grad_first, grad_gain, grad_bias)
    features, grad_conv, grad_first, grad_gain, grad_bias = pl.pallas_call(
        pass_on,
        out_shape=tuple(jax.ShapeDtypeStruct(each.shape, each.dtype) for each in results),
        in_specs=[pl.BlockSpec(memory_space=pl.ANY)] * 5,
        out_specs=[pl.BlockSpec(memory_space=pl.ANY)] * 5,
        scratch_shapes=[pltpu.VMEM(each.shape, each.dtype) for each in results] + [dma((8,)), dma((8,))],
    )(*results)
    return (features.transpose(1, 0, 2), grad_conv, grad_first.T, grad_gain[0], grad_bias[0])


def solution(mesh):
    shape = dict(mesh.shape)
    fused = shape["dp"] == 8 and shape["group"] == 4
    return jax.shard_map(
        local_fused if fused else local,
        mesh=mesh,
        in_specs=(
            P(("dp", "group"), None),
            P(("dp", "group")),
            P(("dp", "group")),
            P("dp", None),
            P(),
            P(),
            P("dp", None),
            P(("dp", "group"), None, None),
        ),
        out_specs=(P(("dp", "group"), None, None), P("dp", None), P("dp", None), P(), P()),
        check_vma=False,
    )
```

```python
import functools

import jax
import jax.numpy as jnp
from jax import lax
from jax.experimental import pallas as pl
from jax.experimental.pallas import tpu as pltpu
from jax.sharding import PartitionSpec as P

MESH = pl.DeviceIdType.MESH
F32, BF16 = jnp.float32, jnp.bfloat16
CHUNK = 32


def gelu_slope(values):
    return (
        0.5 * (1.0 + lax.erf(values * 0.7071067811865476))
        + values * jnp.exp(-0.5 * values * values) * 0.3989422804014327
    )


def tap_matrix(hidden, frames_second):
    row_count, frames_first, channels = hidden.shape
    zero_frame = jnp.zeros((row_count, 1, channels), hidden.dtype)
    paired = jnp.concatenate([hidden, zero_frame], axis=1).reshape(
        row_count, frames_second + 1, 2, channels
    )
    even_half = paired[:, :, 0]
    odd_half = paired[:, :, 1]
    stacked = jnp.concatenate(
        [even_half[:, :frames_second], odd_half[:, :frames_second], even_half[:, 1:]], axis=2
    )
    return stacked.reshape(row_count * frames_second, 3 * channels)


def spread_back(back_taps, row_count, frames_second, frames_first):
    first_tap = back_taps[0].reshape(row_count, frames_second, -1)
    middle_tap = back_taps[1].reshape(row_count, frames_second, -1)
    last_tap = back_taps[2].reshape(row_count, frames_second, -1)
    channels = first_tap.shape[2]
    zero_frame = jnp.zeros((row_count, 1, channels), jnp.float32)
    even_half = jnp.concatenate([first_tap, zero_frame], axis=1) + jnp.concatenate(
        [zero_frame, last_tap], axis=1
    )
    odd_half = jnp.concatenate([middle_tap, zero_frame], axis=1)
    joined = jnp.stack([even_half, odd_half], axis=2).reshape(
        row_count, 2 * frames_second + 2, channels
    )
    return joined[:, :frames_first]


def local(
    waveform, lengths, packing, first_weight, norm_gain, norm_bias, conv_weight, grad_features
):
    row_count, capacity = waveform.shape
    channels = norm_gain.shape[0]
    frames_first = capacity // 5 - 1
    frames_second = (capacity // 5 - 2) // 2
    groups = lax.axis_size("group")
    own_group = lax.axis_index("group")
    group_rows = groups * row_count
    all_pack, all_lengths = (
        lax.all_gather(packing, "group", axis=0, tiled=True),
        lax.all_gather(lengths, "group", axis=0, tiled=True),
    )
    target = all_pack // row_count
    slot_index = all_pack % row_count
    positions = jnp.arange(group_rows)
    source = positions // row_count
    same_source = source[:, None] == source[None, :]
    same_target = target[:, None] == target[None, :]
    before = positions[:, None] > positions[None, :]
    rank_among = jnp.sum((same_source & same_target & before).astype(jnp.int32), axis=1)
    arriving = target == own_group
    slot_ids = jnp.arange(row_count)
    choose_slot = (slot_index[None, :] == slot_ids[:, None]) & arriving[None, :]
    local_lengths = jnp.sum(jnp.where(choose_slot, all_lengths[None, :], 0), axis=1)
    per_peer = 2 * ((row_count + 2 * groups - 1) // (2 * groups))
    lane_ids = jnp.arange(per_peer)
    own_target = lax.dynamic_slice_in_dim(target, own_group * row_count, row_count)
    own_rank = lax.dynamic_slice_in_dim(rank_among, own_group * row_count, row_count)
    outgoing = (
        (own_target[None, None, :] == jnp.arange(groups)[:, None, None])
        & (own_rank[None, None, :] == lane_ids[None, :, None])
    ).astype(jnp.bfloat16)
    send_rows = jnp.einsum(
        "gkr,rs->gks", outgoing, waveform, preferred_element_type=jnp.float32
    ).astype(jnp.bfloat16)
    received = lax.all_to_all(send_rows, "group", split_axis=0, concat_axis=0, tiled=True)
    pick_slots = (
        choose_slot[:, :, None] & (rank_among[None, :, None] == lane_ids[None, None, :])
    ).astype(jnp.float32)
    pick_slots = jnp.sum(pick_slots.reshape(row_count, groups, row_count, per_peer), axis=2).astype(
        jnp.bfloat16
    )
    wave_rows = jnp.einsum(
        "lsk,skn->ln", pick_slots, received, preferred_element_type=jnp.float32
    ).astype(jnp.bfloat16)
    first_whole = lax.all_gather(first_weight, "dp", axis=0, tiled=True)
    in_length = jnp.arange(capacity)[None, :] < local_lengths[:, None]
    masked = jnp.where(in_length, wave_rows, jnp.zeros_like(wave_rows))
    blocks = masked.reshape(row_count, capacity // 5, 5)
    taps_first = jnp.concatenate([blocks[:, :-1], blocks[:, 1:]], axis=2).reshape(
        row_count * frames_first, 10
    )
    conv_first = lax.dot_general(
        taps_first, first_whole, (((1,), (1,)), ((), ())), preferred_element_type=jnp.float32
    )
    conv_first = conv_first.reshape(row_count, frames_first, channels)
    count_first = (local_lengths - 10) // 5 + 1
    count_second = (count_first - 3) // 2 + 1
    valid_first = (jnp.arange(frames_first)[None, :] < count_first[:, None]).astype(jnp.float32)[
        :, :, None
    ]
    valid_second = (jnp.arange(frames_second)[None, :] < count_second[:, None]).astype(jnp.float32)[
        :, :, None
    ]
    count_float = count_first.astype(jnp.float32)[:, None, None]
    row_mean = jnp.sum(conv_first * valid_first, axis=1, keepdims=True) / count_float
    centred = (conv_first - row_mean) * valid_first
    row_var = jnp.sum(centred * centred, axis=1, keepdims=True) / count_float
    inv_scale = lax.rsqrt(row_var + 1e-05)
    normed = (conv_first - row_mean) * inv_scale
    shifted = normed * norm_gain + norm_bias
    hidden = (jax.nn.gelu(shifted, approximate=False) * valid_first).astype(jnp.bfloat16)
    taps_second = tap_matrix(hidden, frames_second)
    conv_whole = lax.all_gather(conv_weight, "dp", axis=0, tiled=True)
    conv_second = lax.dot_general(
        taps_second, conv_whole, (((1,), (1,)), ((), ())), preferred_element_type=jnp.float32
    )
    conv_second = conv_second.reshape(row_count, frames_second, channels)
    features = (jax.nn.gelu(conv_second, approximate=False) * valid_second).astype(jnp.bfloat16)
    delta_second = (
        grad_features.astype(jnp.float32) * valid_second * gelu_slope(conv_second)
    ).astype(jnp.bfloat16)
    delta_flat = delta_second.reshape(row_count * frames_second, channels)
    back_taps = tuple(
        (
            jnp.dot(
                delta_flat,
                conv_whole[:, tap_index * channels : (tap_index + 1) * channels],
                preferred_element_type=jnp.float32,
            )
            for tap_index in range(3)
        )
    )
    share = lax.psum_scatter(
        lax.dot_general(
            delta_flat, taps_second, (((0,), (0,)), ((), ())), preferred_element_type=jnp.float32
        ),
        "dp",
        scatter_dimension=0,
        tiled=True,
    )
    grad_conv = lax.psum(share, "group")
    delta_hidden = spread_back(back_taps, row_count, frames_second, frames_first)
    delta_norm = delta_hidden * valid_first * gelu_slope(shifted)
    gain_term = jnp.sum(delta_norm * normed, axis=(0, 1))
    bias_term = jnp.sum(delta_norm, axis=(0, 1))
    scaled = delta_norm * norm_gain
    mean_grad = jnp.sum(scaled, axis=1, keepdims=True) / count_float
    mean_cross = jnp.sum(scaled * normed, axis=1, keepdims=True) / count_float
    delta_first = ((scaled - mean_grad - normed * mean_cross) * inv_scale * valid_first).astype(
        jnp.bfloat16
    )
    first_term = lax.dot_general(
        delta_first.reshape(row_count * frames_first, channels),
        taps_first,
        (((0,), (0,)), ((), ())),
        preferred_element_type=jnp.float32,
    )
    stacked = jnp.concatenate([first_term, gain_term[:, None], bias_term[:, None]], axis=1)
    summed = lax.psum(stacked, ("dp", "group"))
    shard_rows = channels // lax.axis_size("dp")
    grad_first = lax.dynamic_slice_in_dim(
        summed[:, :10], lax.axis_index("dp") * shard_rows, shard_rows, 0
    )
    return (features, grad_conv, grad_first, summed[:, 10], summed[:, 11])


BLOCKS = ((0, 512), (512, 512), (1024, 512))


def phi_and_slope(values):
    phi = 0.5 + 0.5 * lax.erf(values * 0.7071067811865476)
    return phi, phi + (values * 0.3989422804014327) * jnp.exp2(values * values * -0.7213475204444817)


def fold_rows(block):
    return jnp.sum(block.reshape(block.shape[0] // 8, 8, block.shape[1]), axis=0)


def three_parts(values, out):
    high = values.astype(BF16)
    rest = values - high.astype(F32)
    middle = rest.astype(BF16)
    out[0:16] = high
    out[16:32] = middle
    out[32:48] = (rest - middle.astype(F32)).astype(BF16)


def fused_kernel(
    wave_in, lengths_in, packing_in, first_in, conv_ref, gain_in, bias_in, cot_ref,
    feat_ref, gconv_ref, gfirst_ref, ggain_ref, gbias_ref,
    wave_own, lengths_own, packing_own, first_own, gain_ref, bias_ref, wide, narrow, wave_ref, first_ref, second, in_sem,
    rows_all, first_all, first16, conv_all, turned, slope, taps, even_rows, delta, before, delta_turned,
    cot_wide, cot_rows, feat_wide, feat_rows, lhs_even, lhs_odd, rhs, counts, means, inv_all, gram, cross, acc,
    gc_full, gc_send, gc_r1, gc_k2, gc_s2, gc_r2, gc_k3, gc_s3, gc_r3, gc_out,
    sm_half, sm_core, sm_xy, sm_z, sm_out,
    row_ss, row_rs, first_ss, first_rs, own_ss, fw_ss, conv_rs, own_sem, cot_sem, feat_sem,
    s1_ss, s1_rs, s2_ss, s2_rs, s3_ss, s3_rs, s4_ss, s4_rs,
    sc_ss, sc_rs, sxy_ss, sxy_rs, sz_ss, sz_rs, so_ss, so_rs,
):
    dp, grp = lax.axis_index("dp"), lax.axis_index("group")
    core, xpos = grp % 2, grp // 2
    ypos, zpos = dp % 2, dp // 2
    partner = (dp, xpos * 2 + (1 - core))
    xpeer = (dp, (1 - xpos) * 2 + core)
    ypeer = (zpos * 2 + (1 - ypos), grp)
    corner = (zpos * 2 + (1 - ypos), (1 - xpos) * 2 + core)
    plane = (None, xpeer, ypeer, corner)

    lines = (zpos, zpos + 1 - 2 * (zpos % 2), (zpos + 2) % 4, 3 - zpos)
    near = zpos // 2
    far = 1 - near

    def zpeer(j):
        return lines[j] * 2 + ypos

    def remote(src, dst, ss, rs, dev):
        return pltpu.make_async_remote_copy(
            src_ref=src, dst_ref=dst, send_sem=ss, recv_sem=rs, device_id=dev, device_id_type=MESH
        )

    sends = []

    def send(src, dst, ss, rs, dev):
        c = remote(src, dst, ss, rs, dev)
        c.start()
        sends.append(c)

    def arrived(ref, ss, rs, dev):
        remote(ref, ref, ss, rs, dev).wait_recv()

    cot_in = pltpu.make_async_copy(cot_ref, cot_wide.at[0:255], cot_sem)
    barrier = pltpu.get_barrier_semaphore()
    for j in (3, 2, 1):
        for y_at in (1 - ypos, ypos):
            pl.semaphore_signal(barrier, inc=1, device_id=(lines[j] * 2 + y_at, grp), device_id_type=MESH)
    for device in (corner, ypeer, xpeer, partner, (dp, (1 - xpos) * 2 + 1 - core)):
        pl.semaphore_signal(barrier, inc=1, device_id=device, device_id_type=MESH)
    own = pltpu.make_async_copy(conv_ref, conv_all.at[dp], own_sem)
    own.start()
    loads = []
    pairs = (
        (wave_in, wave_own), (first_in, first_own), (lengths_in, lengths_own), (packing_in, packing_own),
        (gain_in, gain_ref), (bias_in, bias_ref),
    )
    for k, (source, target) in enumerate(pairs):
        c = pltpu.make_async_copy(source, target, in_sem.at[k])
        c.start()
        loads.append(c)
    cot_in.start()
    cot_wide[255] = jnp.zeros((4, 512), BF16)
    even_rows[256:264] = jnp.zeros((8, 512), F32)
    acc[...] = jnp.zeros_like(acc)
    for c in loads:
        c.wait()
    piece = first_own[...].astype(F32)
    piece = jnp.concatenate([piece, jnp.zeros((6, 64), F32)], axis=0)
    piece = jnp.concatenate([piece, piece], axis=1)
    lane = lax.broadcasted_iota(jnp.int32, (16, 128), 1)
    piece = jnp.where(lane // 64 == dp % 2, piece, 0.0).astype(BF16)
    first_ref[...] = piece
    first_all[dp] = piece
    wave = wave_own[...].astype(F32)
    wave = jnp.concatenate([wave, wave], axis=0)
    wide[...] = jnp.concatenate([wave] * 16, axis=0).T
    lane = lax.broadcasted_iota(jnp.int32, (256, 128), 1) // 4
    taken = jnp.zeros((256, 128), F32)
    for k in range(10):
        taken = jnp.where(lane == k, wide[pl.ds(k, 256, stride=10), :], taken)
    narrow[0] = taken[0:128].T
    narrow[1] = taken[128:256].T
    row_ids = lax.broadcasted_iota(jnp.int32, (16, 256), 0)
    for r in range(4):
        place = packing_own[0:1, r : r + 1]
        length = lengths_own[0:1, r : r + 1]
        notes = jnp.where(row_ids == 10, place, jnp.where(row_ids == 11, length // 16, length % 16)).astype(F32)
        block = jnp.concatenate([narrow[0, pl.ds(r, 16, stride=4), :], narrow[1, pl.ds(r, 16, stride=4), :]], axis=1)
        block = jnp.where(row_ids < 10, block, notes).astype(BF16)
        wave_ref[r] = block
        rows_all[grp, r] = block
    pl.semaphore_wait(barrier, 11)

    for j in (3, 2, 1, 0):
        for y_at in (1 - ypos, ypos) if j > 0 else (1 - ypos,):
            peer = (lines[j] * 2 + y_at, grp)
            send(first_ref, first_all.at[dp], first_ss.at[2 * j + (0 if y_at is ypos else 1)], first_rs.at[dp], peer)
    for j in range(1, 4):
        send(wave_ref, rows_all.at[grp], row_ss.at[j], row_rs.at[grp], (dp, (grp + j) % 4))
    mine = conv_ref.at[grp]
    across = (1 - xpos) * 2 + core
    send(mine, conv_all.at[dp, grp], own_ss.at[0], conv_rs.at[dp, grp], ypeer)
    send(mine, conv_all.at[dp, grp], own_ss.at[1], conv_rs.at[dp, grp], (zpeer(1), grp))
    send(conv_ref.at[across], conv_all.at[dp, across], own_ss.at[4], conv_rs.at[dp, across], (zpeer(1), grp))
    for j in (2, 3):
        send(mine, conv_all.at[dp, grp], own_ss.at[j], conv_rs.at[dp, grp], (zpeer(j), grp))
    passed = []

    def pass_on_piece(p, q, devices):
        piece = conv_all.at[p, q]
        arrived(piece, own_ss.at[0], conv_rs.at[p, q], xpeer)
        for device in devices:
            send(piece, piece, fw_ss.at[len(passed)], conv_rs.at[p, q], device)
            passed.append(device)

    def column(j):
        return lines[j] * 2 + 1 - ypos

    cot_in.wait()

    def split_rows(i, _):
        part = pl.ds(pl.multiple_of(i * CHUNK, CHUNK), CHUNK)
        block = cot_wide[part].astype(F32)
        for r in range(4):
            cot_rows[r, part] = block[:, r, :].astype(BF16)
        return 0

    lax.fori_loop(0, 256 // CHUNK, split_rows, 0)

    pass_on_piece(column(0), grp, (xpeer, partner))
    pass_on_piece(zpeer(1), grp, (ypeer, partner))

    for j in range(1, 4):
        p = (grp + j) % 4
        arrived(rows_all.at[p], row_ss.at[j], row_rs.at[p], (dp, p))

    pair_ids = lax.broadcasted_iota(jnp.int32, (16, 256), 1).astype(F32) * 2.0
    for r in range(4):
        place = (grp * 4 + r).astype(F32)
        chosen = jnp.zeros((16, 256), F32)
        for s in range(4):
            for i in range(4):
                row = rows_all[s, i].astype(F32)
                chosen = chosen + row * (row[10:11] == place).astype(F32)
        length = chosen[11:12] * 16.0 + chosen[12:13]
        count = jnp.floor((length - 9.5) * 0.2) + 1.0
        counts[r] = jnp.concatenate([count, count], axis=1)
        one = jnp.where(row_ids == 10, 1.0, 0.0)
        even = jnp.where(row_ids < 10, chosen, one)
        following = pltpu.roll(pltpu.roll(chosen, 255, 1), 5, 0)
        odd = jnp.where(row_ids < 5, pltpu.roll(chosen, 11, 0), jnp.where(row_ids < 10, following, one))
        even = jnp.where(pair_ids < count, even, 0.0).astype(BF16)
        odd = jnp.where(pair_ids + 1.0 < count, odd, 0.0).astype(BF16)
        for k in range(3):
            lhs_even[r, 16 * k : 16 * k + 16] = even
            lhs_odd[r, 16 * k : 16 * k + 16] = odd
        inner = (((1,), (1,)), ((), ()))
        gram[r] = lax.dot_general(even, even, inner, preferred_element_type=F32) + lax.dot_general(
            odd, odd, inner, preferred_element_type=F32
        )

    for j in range(1, 8):
        p = (dp + j) % 8
        arrived(first_all.at[p], first_ss.at[j], first_rs.at[p], (p, grp))
    for b in range(4):
        first16[:, b * 128 : b * 128 + 128] = first_all[2 * b] + first_all[2 * b + 1]

    def front(r, _):
        weights = first16[...].astype(F32)
        gain, bias = gain_ref[...], bias_ref[...]
        inv_count = 1.0 / counts[r]
        tap_sums = gram[r][:, 10:11]
        mean = jnp.sum(weights * tap_sums, axis=0, keepdims=True) * inv_count
        means[r] = mean
        centre = gram[r] - tap_sums * gram[r][10:11, :] * inv_count[:, 0:16]
        high = centre.astype(BF16)
        rest = centre - high.astype(F32)
        middle_part = rest.astype(BF16)
        low = (rest - middle_part.astype(F32)).astype(BF16)
        taps16 = first16[...]
        cross[r] = (
            jnp.dot(high, taps16, preferred_element_type=F32)
            + jnp.dot(middle_part, taps16, preferred_element_type=F32)
        ) + jnp.dot(low, taps16, preferred_element_type=F32)
        ids = lax.broadcasted_iota(jnp.int32, (16, 512), 0)
        three_parts(jnp.where(ids == 10, -mean, weights), rhs)
        turn = (((0,), (0,)), ((), ()))
        total = jnp.zeros((8, 512), F32)
        for lhs in (lhs_even, lhs_odd):
            centred = lax.dot_general(lhs[r], rhs[...], turn, preferred_element_type=F32)
            total = total + fold_rows(centred * centred)
        inv = lax.rsqrt(jnp.sum(total, axis=0, keepdims=True) * inv_count + 1e-05)
        inv_all[r] = inv
        factor = inv * gain
        three_parts(jnp.where(ids == 10, bias - mean * factor, weights * factor), rhs)
        for half, lhs in enumerate((lhs_even, lhs_odd)):
            shifted = lax.dot_general(lhs[r], rhs[...], turn, preferred_element_type=F32)
            for i in range(256 // CHUNK):
                value = shifted[i * CHUNK : (i + 1) * CHUNK]
                phi, grad = phi_and_slope(value)
                hidden = value * phi
                rows = pl.ds(pl.multiple_of(r * 256 + i * CHUNK, CHUNK), CHUNK)
                slope[rows, half * 512 : half * 512 + 512] = grad.astype(BF16)
                taps[rows, half * 512 : half * 512 + 512] = hidden.astype(BF16)
                if half == 0:
                    even_rows[i * CHUNK : (i + 1) * CHUNK] = hidden
        all_rows = pl.ds(pl.multiple_of(r * 256, 256), 256)
        taps[all_rows, 1024:1536] = even_rows[1:257].astype(BF16)
        return 0

    pass_on_piece(zpeer(1), across, (ypeer, partner))
    lax.fori_loop(0, 1, front, 0)
    for j in (2, 3):
        pass_on_piece(zpeer(j), grp, (corner, ypeer, xpeer, partner))
    lax.fori_loop(1, 2, front, 0)
    pass_on_piece(column(0), across, (partner,))
    pass_on_piece(column(1), grp, (partner,))
    lax.fori_loop(2, 3, front, 0)
    pass_on_piece(column(1), across, (partner,))
    lax.fori_loop(3, 4, front, 0)
    own.wait()

    def from_partner(places):
        for p in places:
            for q in (xpos * 2 + 1 - core, (1 - xpos) * 2 + 1 - core):
                arrived(conv_all.at[p, q], own_ss.at[0], conv_rs.at[p, q], partner)

    even_rows[0:8] = jnp.zeros((8, 512), F32)

    def middle(half):
        lanes = pl.ds(pl.multiple_of(half * 256, 256), 256)
        for k in range(2):
            turned[half, :, k * 128 : k * 128 + 128] = (
                conv_all[pl.ds(4 * half + 2 * k, 2)].reshape(128, 1536).T
            )
        for r in range(4):
            rows = slice(r * 256, r * 256 + 256)
            second[rows] = jnp.dot(taps[rows], turned[half], preferred_element_type=F32)

        ids = lax.broadcasted_iota(jnp.int32, (CHUNK, 256), 0).astype(F32)
        for r in range(4):
            all_rows = slice(r * 256, r * 256 + 256)
            count2 = jnp.floor((counts[r][:, 0:256] - 2.5) * 0.5) + 1.0
            for i in range(256 // CHUNK):
                valid = ids + float(i * CHUNK) < count2
                rows = slice(r * 256 + i * CHUNK, r * 256 + (i + 1) * CHUNK)
                value = second[rows]
                phi, grad = phi_and_slope(value)
                part = slice(i * CHUNK, (i + 1) * CHUNK)
                feat_rows[r, part, lanes] = jnp.where(valid, value * phi, 0.0).astype(BF16)
                back = jnp.where(valid, cot_rows[r, part, lanes].astype(F32) * grad, 0.0)
                delta[rows, lanes] = back.astype(BF16)
                even_rows[8 + i * CHUNK : 8 + (i + 1) * CHUNK, lanes] = back
            before[all_rows, lanes] = even_rows[7:263, lanes].astype(BF16)
            delta_turned[lanes, all_rows] = delta[all_rows, lanes].T

    stage = {}
    halves = (near, far)

    def weight_grad(k, b):
        half = halves[k]
        first, width = BLOCKS[b]
        cols = slice(first, first + width)
        lanes = pl.ds(pl.multiple_of(half * 256, 256), 256)
        part = jnp.dot(delta_turned[lanes, :], taps[:, cols], preferred_element_type=F32)
        part = part.reshape(4, 2, 2, 16, width)
        own_dp = pl.ds(half * 4, 4)
        gc_full[own_dp, :, :, :, cols] = part
        gc_send[own_dp, :, :, :, cols] = part.astype(BF16)
        stage[k, b] = remote(
            gc_send.at[own_dp, :, 1 - core, :, cols],
            gc_r1.at[own_dp, :, :, cols],
            s1_ss.at[k, b],
            s1_rs.at[k, b],
            partner,
        )
        stage[k, b].start()

    def reduce_core(k, b):
        half = halves[k]
        first, width = BLOCKS[b]
        cols = slice(first, first + width)
        stage[k, b].wait()
        for j in (3, 1, 2, 0):
            x_at = xpos if j % 2 == 0 else 1 - xpos
            y_at = ypos if j // 2 == 0 else 1 - ypos
            for step in range(2):
                z = half * 2 + step
                d = z * 2 + y_at
                total = gc_full[d, x_at, core, :, cols] + gc_r1[d, x_at, :, cols].astype(F32)
                if j == 0:
                    gc_k2[z, :, cols] = total
                else:
                    gc_s2[j, z, :, cols] = total.astype(BF16)
            if j > 0:
                pair = pl.ds(half * 2, 2)
                send(
                    gc_s2.at[j, pair, :, cols],
                    gc_r2.at[j, pair, :, cols],
                    s2_ss.at[k, b, j],
                    s2_rs.at[k, b, j],
                    plane[j],
                )

    def reduce_plane(k, b):
        half = halves[k]
        first, width = BLOCKS[b]
        cols = slice(first, first + width)
        pair = pl.ds(half * 2, 2)
        for j in range(1, 4):
            arrived(gc_r2.at[j, pair, :, cols], s2_ss.at[k, b, j], s2_rs.at[k, b, j], plane[j])
        for step in range(2):
            z = half * 2 + step
            total = gc_k2[z, :, cols]
            for j in range(1, 4):
                total = total + gc_r2[j, z, :, cols].astype(F32)
            gc_k3[z, :, cols] = total
            gc_s3[z, :, cols] = total.astype(BF16)
        for j in (1,) if k == 0 else (2, 3):
            zp = lines[j]
            send(
                gc_s3.at[zp, :, cols],
                gc_r3.at[zpos, :, cols],
                s3_ss.at[b, j],
                s3_rs.at[b, zpos],
                (zp * 2 + ypos, grp),
            )

    def reduce_line(b):
        first, width = BLOCKS[b]
        cols = slice(first, first + width)
        total = gc_k3[zpos, :, cols]
        for j in range(1, 4):
            zp = lines[j]
            arrived(gc_r3.at[zp, :, cols], s3_ss.at[b, j], s3_rs.at[b, zp], (zp * 2 + ypos, grp))
            total = total + gc_r3[zp, :, cols].astype(F32)
        gc_out[grp, :, cols] = total.astype(BF16)
        for j in range(1, 4):
            piece = gc_out.at[grp, :, cols]
            send(piece, piece, s4_ss.at[b, j], s4_rs.at[b, grp], (dp, (grp + j) % 4))

    def gathered(b):
        first, width = BLOCKS[b]
        cols = slice(first, first + width)
        for j in range(1, 4):
            p = (grp + j) % 4
            arrived(gc_out.at[p, :, cols], s4_ss.at[b, j], s4_rs.at[b, p], (dp, p))
        gconv_ref[:, cols] = gc_out[:, :, cols].astype(F32).reshape(64, width)

    def backward(r):
        rows = slice(r * 256, r * 256 + 256)
        weights = conv_all[...].reshape(512, 1536)
        even = jnp.dot(delta[rows, :], weights[:, 0:512], preferred_element_type=F32) + jnp.dot(
            before[rows, :], weights[:, 1024:1536], preferred_element_type=F32
        )
        odd = jnp.dot(delta[rows, :], weights[:, 512:1024], preferred_element_type=F32)
        even = (even * slope[rows, 0:512].astype(F32)).astype(BF16)
        odd = (odd * slope[rows, 512:1024].astype(F32)).astype(BF16)
        found = jnp.dot(lhs_even[r, 0:16], even, preferred_element_type=F32) + jnp.dot(
            lhs_odd[r, 0:16], odd, preferred_element_type=F32
        )
        inv_count, inv, mean = 1.0 / counts[r], inv_all[r], means[r]
        plain = found[10:11]
        with_normed = inv * (
            jnp.sum(first16[...].astype(F32) * found, axis=0, keepdims=True) - mean * plain
        )
        tap_sums = gram[r][:, 10:11]
        grads = (inv * gain_ref[...]) * (
            found - tap_sums * (plain * inv_count) - cross[r] * (with_normed * inv * inv_count)
        )
        ids = lax.broadcasted_iota(jnp.int32, (16, 512), 0)
        grads = jnp.where(ids == 10, with_normed, jnp.where(ids == 11, plain, grads))
        acc[...] += grads

    blocks = range(len(BLOCKS))
    from_partner((column(0), zpeer(1), column(1)))
    middle(near)
    for j in (2, 3):
        pass_on_piece(zpeer(j), across, (partner,))
        pass_on_piece(column(j), grp, (partner,))
        pass_on_piece(column(j), across, (partner,))
    for b in blocks:
        weight_grad(0, b)
        if b > 0:
            reduce_core(0, b - 1)
    from_partner((zpeer(2), zpeer(3), column(2), column(3)))
    reduce_core(0, len(BLOCKS) - 1)
    middle(far)
    for b in blocks:
        weight_grad(1, b)
        if b > 0:
            reduce_core(1, b - 1)
    backward(0)
    reduce_core(1, len(BLOCKS) - 1)
    backward(1)
    backward(2)
    reduce_plane(0, 0)
    backward(3)
    reduce_plane(0, 1)

    total = acc[...]
    sm_half[0] = total[:, 0:256]
    sm_half[1] = total[:, 256:512]
    small = remote(sm_half.at[1 - core], sm_core, sc_ss, sc_rs, partner)
    small.start()
    small.wait()
    here = xpos * 2 + ypos
    sm_xy[here] = sm_half[core] + sm_core[...]
    for j in range(1, 4):
        send(sm_xy.at[here], sm_xy.at[here], sxy_ss.at[j], sxy_rs.at[j], plane[j])

    def join_rows(i, _):
        part = pl.ds(pl.multiple_of(i * CHUNK, CHUNK), CHUNK)
        parts = [feat_rows[r, part].astype(F32) for r in range(4)]
        feat_wide[part] = jnp.stack(parts, axis=1).astype(BF16)
        return 0

    reduce_plane(0, 2)
    for b in blocks:
        reduce_plane(1, b)
    lax.fori_loop(0, 256 // CHUNK, join_rows, 0)
    feat_out = pltpu.make_async_copy(feat_wide.at[0:255], feat_ref, feat_sem)
    feat_out.start()
    there = ((1 - xpos) * 2 + ypos, xpos * 2 + 1 - ypos, (1 - xpos) * 2 + 1 - ypos)
    for j in range(1, 4):
        arrived(sm_xy.at[there[j - 1]], sxy_ss.at[j], sxy_rs.at[j], plane[j])
    sm_z[zpos] = (sm_xy[0] + sm_xy[1]) + (sm_xy[2] + sm_xy[3])
    for j in (3, 2, 1):
        zp = lines[j]
        send(sm_z.at[zpos], sm_z.at[zpos], sz_ss.at[j], sz_rs.at[zpos], (zp * 2 + ypos, grp))
    for b in blocks:
        reduce_line(b)
    for j in range(1, 4):
        zp = (zpos + j) % 4
        arrived(sm_z.at[zp], sz_ss.at[j], sz_rs.at[zp], (zp * 2 + ypos, grp))
    sm_out[core] = (sm_z[0] + sm_z[1]) + (sm_z[2] + sm_z[3])
    last = remote(sm_out.at[core], sm_out.at[core], so_ss, so_rs.at[core], partner)
    last.start()
    for b in range(len(BLOCKS)):
        gathered(b)
    arrived(sm_out.at[1 - core], so_ss, so_rs.at[1 - core], partner)
    small_sum = jnp.concatenate([sm_out[0], sm_out[1]], axis=1)
    ggain_ref[...] = small_sum[10:11]
    gbias_ref[...] = small_sum[11:12]
    gfirst_ref[...] = pltpu.roll(small_sum, (8 - dp) % 8 * 64, 1)[0:10, 0:64]
    feat_out.wait()
    last.wait_send()
    for c in sends:
        c.wait_send()


def pass_on(*refs):
    sources, targets, buffers, (in_sem, out_sem) = refs[0:5], refs[5:10], refs[10:15], refs[15:17]
    spans = [(0, pl.ds(0, 64)), (0, pl.ds(64, 64)), (0, pl.ds(128, 64)), (0, pl.ds(192, 63))]
    views = [tuple(group[k].at[span] for group in (sources, buffers, targets)) for k, span in spans]
    views += [(sources[k], buffers[k], targets[k]) for k in range(1, 5)]
    reads, writes = [], []
    for k, (source, buffer, target) in enumerate(views):
        c = pltpu.make_async_copy(source, buffer, in_sem.at[k])
        c.start()
        reads.append(c)
    for k, (source, buffer, target) in enumerate(views):
        reads[k].wait()
        c = pltpu.make_async_copy(buffer, target, out_sem.at[k])
        c.start()
        writes.append(c)
    for c in writes:
        c.wait()


def local_fused(
    waveform, lengths, packing, first_weight, norm_gain, norm_bias, conv_weight, grad_features
):
    vmem = lambda *shape: pltpu.VMEM(shape, F32)
    vmem16 = lambda *shape: pltpu.VMEM(shape, BF16)
    dma = pltpu.SemaphoreType.DMA
    n = len(BLOCKS)
    features, grad_conv, grad_first, grad_gain, grad_bias = pl.pallas_call(
        fused_kernel,
        out_shape=(
            jax.ShapeDtypeStruct((255, 4, 512), BF16),
            jax.ShapeDtypeStruct((64, 1536), F32),
            jax.ShapeDtypeStruct((10, 64), F32),
            jax.ShapeDtypeStruct((1, 512), F32),
            jax.ShapeDtypeStruct((1, 512), F32),
        ),
        in_specs=[pl.BlockSpec(memory_space=pl.ANY)] * 8,
        out_specs=[pl.BlockSpec(memory_space=pl.ANY)] + [pl.BlockSpec(memory_space=pltpu.VMEM)] * 4,
        scratch_shapes=[
            vmem16(4, 2560), pltpu.VMEM((1, 4), jnp.int32), pltpu.VMEM((1, 4), jnp.int32), vmem16(10, 64),
            vmem(1, 512), vmem(1, 512), vmem(2560, 128), vmem(2, 128, 128), vmem16(4, 16, 256), vmem16(16, 128),
            vmem(1024, 256), dma((6,)),
            vmem16(4, 4, 16, 256), vmem16(8, 16, 128), vmem16(16, 512), vmem16(8, 4, 16, 1536), vmem16(2, 1536, 256),
            vmem16(1024, 1024), vmem16(1024, 1536), vmem(264, 512), vmem16(1024, 512), vmem16(1024, 512),
            vmem16(512, 1024),
            vmem16(256, 4, 512), vmem16(4, 256, 512), vmem16(256, 4, 512), vmem16(4, 256, 512),
            vmem16(4, 48, 256), vmem16(4, 48, 256), vmem16(48, 512), vmem(4, 1, 512), vmem(4, 1, 512),
            vmem(4, 1, 512), vmem(4, 16, 16), vmem(4, 16, 512), vmem(16, 512),
            vmem(8, 2, 2, 16, 1536), vmem16(8, 2, 2, 16, 1536), vmem16(8, 2, 16, 1536),
            vmem(4, 16, 1536), vmem16(4, 4, 16, 1536), vmem16(4, 4, 16, 1536),
            vmem(4, 16, 1536), vmem16(4, 16, 1536), vmem16(4, 16, 1536), vmem16(4, 16, 1536),
            vmem(2, 16, 256), vmem(16, 256), vmem(4, 16, 256), vmem(4, 16, 256), vmem(2, 16, 256),
            dma((4,)), dma((4,)), dma((8,)), dma((8,)), dma((5,)), dma((24,)), dma((8, 4)),
            dma, dma, dma,
            dma((2, n)), dma((2, n)), dma((2, n, 4)), dma((2, n, 4)), dma((n, 4)), dma((n, 4)), dma((n, 4)), dma((n, 4)),
            dma, dma, dma((4,)), dma((4,)), dma((4,)), dma((4,)), dma, dma((2,)),
        ],
        compiler_params=pltpu.CompilerParams(
            collective_id=0, has_side_effects=True, vmem_limit_bytes=60 * 1024 * 1024
        ),
    )(
        waveform, lengths[None], packing[None], first_weight.T, conv_weight.reshape(4, 16, 1536),
        norm_gain[None], norm_bias[None], grad_features.transpose(1, 0, 2),
    )
    results = (features, grad_conv, grad_first, grad_gain, grad_bias)
    features, grad_conv, grad_first, grad_gain, grad_bias = pl.pallas_call(
        pass_on,
        out_shape=tuple(jax.ShapeDtypeStruct(each.shape, each.dtype) for each in results),
        in_specs=[pl.BlockSpec(memory_space=pl.ANY)] * 5,
        out_specs=[pl.BlockSpec(memory_space=pl.ANY)] * 5,
        scratch_shapes=[pltpu.VMEM(each.shape, each.dtype) for each in results] + [dma((8,)), dma((8,))],
    )(*results)
    return (features.transpose(1, 0, 2), grad_conv, grad_first.T, grad_gain[0], grad_bias[0])


def solution(mesh):
    shape = dict(mesh.shape)
    fused = shape["dp"] == 8 and shape["group"] == 4
    return jax.shard_map(
        local_fused if fused else local,
        mesh=mesh,
        in_specs=(
            P(("dp", "group"), None),
            P(("dp", "group")),
            P(("dp", "group")),
            P("dp", None),
            P(),
            P(),
            P("dp", None),
            P(("dp", "group"), None, None),
        ),
        out_specs=(P(("dp", "group"), None, None), P("dp", None), P("dp", None), P(), P()),
        check_vma=False,
    )
```
